256 devices in a mesh: member: 8 (over x, core), lat: 8 (over z_hi, y), lon: 4 (over z_lo).
Axes of the slice: x: 4, y: 4, z: 8 (z_hi: 2, z_lo: 4; z = z_hi * 4 + z_lo), core: 2. Of those that a mesh axis runs over, the one named last changes fastest.
Arguments:
- fields: bfloat16 [8, 240, 480, 384], P('member', 'lat', 'lon'), may hold values from -6 to 6
- targets: float32 [73, 240, 480], P(None, 'lat', 'lon'), may hold values from -6 to 6
- filt_re: float32 [8, 240, 384], P('member', 'lon', 'lat'), may hold values from -6 to 6
- filt_im: float32 [8, 240, 384], P('member', 'lon', 'lat'), may hold values from -6 to 6
- w_in: bfloat16 [8, 384, 384], P('member'), may hold values from -0.3125 to 0.3125
- b_in: float32 [8, 384], P('member'), may hold values from -3 to 3
- w_out: bfloat16 [8, 73, 384], P('member'), may hold values from -0.3125 to 0.3125
- b_out: float32 [8, 73], P('member'), may hold values from -6 to 6
Outputs:
- nll: float32 [73, 240, 480], P(None, 'lat', 'lon')
- grad_re: float32 [8, 240, 384], P('member', 'lon', 'lat')
- grad_im: float32 [8, 240, 384], P('member', 'lon', 'lat')
The draws below stay inside these ranges and needn't reach their ends.
All inputs are finite; a program needn't handle non-finite values.
Results may differ from the reference program's by a relative error of at most 0.02.
Values may be sent and summed in bfloat16 or wider, within the bound.
A program may use at most 128 MiB of HBM per device.

```python
import jax
import jax.numpy as jnp
from jax import lax

C = 384
V = 73
NLAT = 240
NLON = 480
MEMBERS = 8
KL = 240


def block_levels(rng, shape, pieces, low, top_value):
    def one(dim, blocks):
        steps = jax.random.uniform(jax.random.fold_in(jax.random.fold_in(rng, 6), dim), (blocks,), jnp.float32, low / len(pieces), top_value / len(pieces))
        return jnp.repeat(jnp.exp(steps), shape[dim] // blocks).reshape((-1,) + (1,) * (len(shape) - dim - 1))

    gain = one(*pieces[0])
    for cut in pieces[1:]:
        gain = gain * one(*cut)
    return gain


def scatter_about(own_key, shape, deviation, reach, pieces=(), kind=jnp.bfloat16):
    array = deviation * jax.random.normal(own_key, shape, jnp.float32)
    if pieces:
        array = array * block_levels(own_key, shape, pieces, -0.22, 0.18)
    return jnp.clip(array, -reach, reach).astype(kind)


def setup_inputs(seed: int = 0) -> dict:
    key_list = jax.random.split(jax.random.key(seed), 9)
    return {
        "fields": scatter_about(key_list[0], (MEMBERS, NLAT, NLON, C), 1.0, 6.0, ((0, 8), (1, 8), (2, 4))),
        "targets": scatter_about(key_list[1], (V, NLAT, NLON), 1.0, 6.0, ((1, 8), (2, 4)), jnp.float32),
        "filt_re": scatter_about(key_list[2], (MEMBERS, KL, C), 1.0, 6.0, ((0, 8), (1, 4), (2, 8)), jnp.float32),
        "filt_im": scatter_about(key_list[3], (MEMBERS, KL, C), 1.0, 6.0, ((0, 8), (1, 4), (2, 8)), jnp.float32),
        "w_in": scatter_about(key_list[4], (MEMBERS, C, C), C ** -0.5, 0.3125, ((0, 8),)),
        "b_in": scatter_about(key_list[5], (MEMBERS, C), 0.5, 3.0, ((0, 8),), jnp.float32),
        "w_out": scatter_about(key_list[6], (MEMBERS, V, C), C ** -0.5, 0.3125, ((0, 8),)),
        "b_out": scatter_about(key_list[7], (MEMBERS, V), 1.0, 6.0, ((0, 8),), jnp.float32),
    }


variance_floor = 0.1

def lat_table(rows):
    degree = jnp.arange(rows, dtype=jnp.float32)[:, None]
    column = jnp.arange(rows, dtype=jnp.float32)[None, :]
    scale = jnp.where(degree == 0, jnp.sqrt(1.0 / rows), jnp.sqrt(2.0 / rows))
    return (scale * jnp.cos(jnp.pi * degree * (column + 0.5) / rows)).astype(jnp.bfloat16)

def lon_table(columns):
    half_modes = columns // 2
    place = jnp.arange(columns, dtype=jnp.int32)[:, None]
    order = jnp.arange(half_modes, dtype=jnp.int32)[None, :]
    angle = 2.0 * jnp.pi * (place * order % columns).astype(jnp.float32) / columns
    scale = jnp.where(order == 0, jnp.sqrt(1.0 / columns), jnp.sqrt(2.0 / columns))
    return jnp.concatenate([scale * jnp.cos(angle), -scale * jnp.sin(angle)], axis=1).astype(jnp.bfloat16)

def mode_mask(first_degree, degrees, half_modes):
    degree = first_degree + jnp.arange(degrees, dtype=jnp.int32)
    order = jnp.arange(2 * half_modes, dtype=jnp.int32) % half_modes
    return (degree[:, None] >= order[None, :]).astype(jnp.float32)

def to_spectral(grid_field, lat_basis, lon_basis):
    rows, columns, width = grid_field.shape
    coef = jnp.dot(lat_basis, grid_field.reshape(rows, columns * width), preferred_element_type=jnp.float32).astype(jnp.bfloat16)
    coef = coef.reshape(rows, columns, width).transpose(0, 2, 1).reshape(rows * width, columns)
    spectrum = jnp.dot(coef, lon_basis, preferred_element_type=jnp.float32)
    return spectrum.reshape(rows, width, columns).transpose(0, 2, 1)

def from_spectral(filtered, lat_basis, lon_basis):
    rows, modes, width = filtered.shape
    flat = filtered.transpose(0, 2, 1).reshape(rows * width, modes)
    back = jnp.dot(flat, lon_basis.T, preferred_element_type=jnp.float32).astype(jnp.bfloat16)
    back = back.reshape(rows, width, modes).transpose(0, 2, 1).reshape(rows, modes * width)
    spatial = jnp.dot(lat_basis.T, back, preferred_element_type=jnp.float32).astype(jnp.bfloat16)
    return spatial.reshape(rows, modes, width)

def apply_filter(spectrum, weight_re, weight_im, keep_modes):
    half_modes = spectrum.shape[1] // 2
    spec_re = spectrum[:, :half_modes]
    spec_im = spectrum[:, half_modes:]
    keep_half = keep_modes[:, :half_modes, None]
    wre = weight_re[:, None, :]
    wim = weight_im[:, None, :]
    out_re = keep_half * (wre * spec_re - wim * spec_im)
    out_im = keep_half * (wre * spec_im + wim * spec_re)
    return jnp.concatenate([out_re, out_im], axis=1).astype(jnp.bfloat16)

def filter_grads(spectrum, g_spec, keep_modes):
    half_modes = spectrum.shape[1] // 2
    keep_half = keep_modes[:, :half_modes, None]
    spec_re = spectrum[:, :half_modes]
    spec_im = spectrum[:, half_modes:]
    grad_sre = g_spec[:, :half_modes]
    grad_sim = g_spec[:, half_modes:]
    grad_wre = lax.optimization_barrier(jnp.sum(keep_half * (grad_sre * spec_re + grad_sim * spec_im), axis=1))
    grad_wim = lax.optimization_barrier(jnp.sum(keep_half * (grad_sim * spec_re - grad_sre * spec_im), axis=1))
    return (grad_wre, grad_wim)

def member_forward(grid_field, weight_re, weight_im, w_first, b_first, w_second, b_second, lat_basis, lon_basis, keep_modes):
    spectrum = to_spectral(grid_field, lat_basis, lon_basis)
    filtered = apply_filter(spectrum, weight_re, weight_im, keep_modes)
    spatial = from_spectral(filtered, lat_basis, lon_basis)
    mixed = (grid_field.astype(jnp.float32) + spatial.astype(jnp.float32)).astype(jnp.bfloat16)
    cells = mixed.reshape(-1, mixed.shape[-1])
    preact = jnp.dot(cells, w_first, preferred_element_type=jnp.float32) + b_first
    hidden = jax.nn.silu(preact).astype(jnp.bfloat16)
    predicted = jnp.dot(w_second, hidden.T, preferred_element_type=jnp.float32) + b_second[:, None]
    return (spectrum, preact, predicted.reshape(w_second.shape[0], grid_field.shape[0], grid_field.shape[1]))

def reference(fields, targets, filt_re, filt_im, w_in, b_in, w_out, b_out):
    rows = fields.shape[1]
    columns = fields.shape[2]
    members = fields.shape[0]
    variables = targets.shape[0]
    lat_basis = lat_table(rows)
    lon_basis = lon_table(columns)
    keep_modes = mode_mask(0, rows, columns // 2)

    def forward_pred(member_args):
        return member_forward(*member_args, lat_basis, lon_basis, keep_modes)[2]
    predicted = lax.map(forward_pred, (fields, filt_re, filt_im, w_in, b_in, w_out, b_out))
    first_sum = lax.optimization_barrier(jnp.sum(predicted, axis=0))
    second_sum = lax.optimization_barrier(jnp.sum(predicted * predicted, axis=0))
    ens_mean = first_sum / members
    variance = second_sum / members - ens_mean * ens_mean + variance_floor
    residual = targets - ens_mean
    inv_var = 1.0 / variance
    nll = 0.5 * (jnp.log(variance) + residual * residual * inv_var)

    def member_backward(member_args):
        grid_field, weight_re, weight_im, w_first, b_first, w_second, b_second = member_args
        spectrum, preact, own_pred = member_forward(grid_field, weight_re, weight_im, w_first, b_first, w_second, b_second, lat_basis, lon_basis, keep_modes)
        g_pred = (-residual * inv_var / members + (inv_var - residual * residual * inv_var * inv_var) * (own_pred - ens_mean) / members) / variables
        flat_grad = g_pred.reshape(variables, -1)
        g_hidden = jnp.dot(flat_grad.T, w_second.astype(jnp.float32), precision=lax.Precision.HIGHEST)
        sigma = jax.nn.sigmoid(preact)
        g_preact = (g_hidden * sigma * (1.0 + preact * (1.0 - sigma))).astype(jnp.bfloat16)
        g_mixed = jnp.dot(g_preact, w_first.T, preferred_element_type=jnp.float32).astype(jnp.bfloat16)
        g_spec = to_spectral(g_mixed.reshape(grid_field.shape), lat_basis, lon_basis)
        return filter_grads(spectrum, g_spec, keep_modes)
    grad_re, grad_im = lax.map(member_backward, (fields, filt_re, filt_im, w_in, b_in, w_out, b_out))
    return (nll, grad_re, grad_im)
```

```python
import functools

import jax
import jax.numpy as jnp
import numpy as np
from jax import lax
from jax.experimental import pallas as pl
from jax.experimental.pallas import tpu as pltpu
from jax.sharding import PartitionSpec as P

MESH_ID = pl.DeviceIdType.MESH
F32 = jnp.float32
BF16 = jnp.bfloat16

rows, columns, width, variables, members = 240, 480, 384, 73, 8
own_rows, own_columns, own_width = 30, 120, 12
chunks = 3
chunk = own_width // chunks
variance_floor = 0.1


def tables():
    k = np.arange(rows, dtype=np.float64)[:, None]
    j = np.arange(rows, dtype=np.float64)[None, :]
    lat = np.where(k == 0, np.sqrt(1.0 / rows), np.sqrt(2.0 / rows)) * np.cos(
        np.pi * k * (j + 0.5) / rows
    )
    half = columns // 2
    place = np.arange(columns, dtype=np.int64)[:, None]
    order = np.arange(half, dtype=np.int64)[None, :]
    angle = 2.0 * np.pi * (place * order % columns).astype(np.float64) / columns
    scale = np.where(order == 0, np.sqrt(1.0 / columns), np.sqrt(2.0 / columns))
    kpad = (np.arange(rows) // 60) * 64 + np.arange(rows) % 60
    jpad = (np.arange(rows) // 30) * 32 + np.arange(rows) % 30
    lpad = (np.arange(columns) // 120) * 128 + np.arange(columns) % 120
    lat_pad = np.zeros((256, 256), np.float32)
    lat_pad[np.ix_(kpad, jpad)] = lat
    lon_pad = np.zeros((512, 512), np.float32)
    lon_pad[np.ix_(lpad, np.arange(half))] = scale * np.cos(angle)
    lon_pad[np.ix_(lpad, 256 + np.arange(half))] = -scale * np.sin(angle)
    return lat_pad, lon_pad


def mm(a, b):
    return jnp.dot(a, b, preferred_element_type=F32)


def wait_for(ref, sem):
    pltpu.make_async_copy(ref, ref, sem).wait()


def kernel(
    fields, targets, filters, w, w_t, b, wo, wo_t, bo, lat, lat_t, lon, lon_t,
    nll, grads,
    cells, fields_t, block, grid, spatial, back, spectrum, preact, pred, pred_in, sums, ggrid,
    weights, gsum, gsum_in, mixed, gpair,
    out_sem, in_sem, back_out, back_in, gout_sem, gin_sem, pred_out, pred_in_sem,
    sums_out, sums_in, fwd_out, fwd_in, filt_out, filt_in, grad_out, grad_in,
):
    im = lax.axis_index("member")
    ilat = lax.axis_index("lat")
    ilon = lax.axis_index("lon")
    me = ilat * 4 + ilon
    partner = (im // 2) * 2 + 1 - im % 2

    def peer(o):
        y, z = ilat % 4, (ilat // 4) * 4 + ilon
        y2, z2 = (y + o % 4) % 4, (z + o // 4) % 8
        la, lo = (z2 // 4) * 4 + y2, z2 % 4
        return (im, la, lo), la, lo

    def at_member(m):
        return (m, ilat, ilon)

    barrier = pltpu.get_barrier_semaphore()

    @pl.loop(1, 32)
    def _(o):
        pl.semaphore_signal(barrier, 1, device_id=peer(o)[0], device_id_type=MESH_ID)

    @pl.loop(1, 8)
    def _(o):
        pl.semaphore_signal(
            barrier, 1, device_id=at_member((im + o) % 8), device_id_type=MESH_ID
        )

    def grid_part(ref, ch, la, lo):
        return ref.at[
            pl.ds(ch * chunk, chunk),
            pl.ds(pl.multiple_of(la * 32, 32), 32),
            pl.ds(pl.multiple_of(lo * 128, 128), 128),
        ]

    def block_part(ref, ch, la, lo):
        return ref.at[pl.ds((la * 4 + lo) * own_width + ch * chunk, chunk)]

    @pl.loop(0, own_rows)
    def _(j):
        x = fields[j].astype(F32)
        x = jnp.concatenate([x, jnp.zeros((8, width), F32)], axis=0).T
        cells[pl.ds(j, width, stride=32), :] = x
        fields_t[j // 4, :, pl.ds(pl.multiple_of((j % 4) * 128, 128), 128)] = x.astype(BF16)

    for j in (30, 31):
        cells[pl.ds(j, width, stride=32), :] = jnp.zeros((width, 128), F32)
    fields_t[7, :, 256:512] = jnp.zeros((width, 256), BF16)

    def fill_block():
        @pl.loop(0, width // 8)
        def _(i):
            part = cells[pl.ds(pl.multiple_of(i * 256, 256), 256), :]
            block[pl.ds(i * 8, 8)] = part.astype(BF16).reshape(8, 32, 128)

    fill_block()
    pl.semaphore_wait(barrier, 31 + 7)

    def filter_copy(o):
        lo = (ilon + o) % 4
        return pltpu.make_async_remote_copy(
            filters,
            weights.at[:, pl.ds(pl.multiple_of(ilon * 64, 64), 64), :],
            filt_out,
            filt_in,
            device_id=(im, ilat, lo),
            device_id_type=MESH_ID,
        )

    @pl.loop(1, 4)
    def _(o):
        filter_copy(o).start()

    weights[:, pl.ds(pl.multiple_of(ilon * 64, 64), 64), :] = filters[...]

    def send_blocks(target, sems_out, sems_in):
        for ch in range(chunks):

            @pl.loop(1, 32)
            def _(o):
                dev, la, lo = peer(o)
                pltpu.make_async_remote_copy(
                    block_part(block, ch, la, lo),
                    grid_part(target, ch, ilat, ilon),
                    sems_out.at[ch],
                    sems_in.at[ch],
                    device_id=dev,
                    device_id_type=MESH_ID,
                ).start()

            target[
                pl.ds(ch * chunk, chunk),
                pl.ds(pl.multiple_of(ilat * 32, 32), 32),
                pl.ds(pl.multiple_of(ilon * 128, 128), 128),
            ] = block[pl.ds(me * own_width + ch * chunk, chunk)]

    def of_31(ref):
        return ref.at[pl.ds(0, 31 * chunk)]

    send_blocks(grid, out_sem, in_sem)
    wait_for(weights.at[:, pl.ds(0, 192), :], filt_in)

    lane = lax.broadcasted_iota(jnp.int32, (256, 128), 1)
    k_row = lax.broadcasted_iota(jnp.int32, (256, 256), 0)
    keep = (k_row // 64) * 60 + k_row % 64 >= lax.broadcasted_iota(jnp.int32, (256, 256), 1)

    def to_spectral(x):
        return mm(mm(lat[...], x).astype(BF16), lon[...])

    for ch in range(chunks):
        wait_for(of_31(block), in_sem.at[ch])

        @pl.loop(ch * chunk, (ch + 1) * chunk)
        def _(c):
            own = lane == ilon * own_width + c
            wr = jnp.sum(jnp.where(own, weights[0], 0.0), axis=1, keepdims=True)
            wi = jnp.sum(jnp.where(own, weights[1], 0.0), axis=1, keepdims=True)
            spectrum[c] = to_spectral(grid[c])
            sr, si = spectrum[c, :, 0:256], spectrum[c, :, 256:512]
            fr = jnp.where(keep, wr * sr - wi * si, 0.0).astype(BF16)
            fi = jnp.where(keep, wr * si + wi * sr, 0.0).astype(BF16)
            lon_back = mm(jnp.concatenate([fr, fi], axis=1), lon_t[...]).astype(BF16)
            spatial[c] = mm(lat_t[...], lon_back).astype(BF16)

        @pl.loop(1, 32)
        def _(o):
            dev, la, lo = peer(o)
            pltpu.make_async_remote_copy(
                grid_part(spatial, ch, la, lo),
                block_part(back, ch, ilat, ilon),
                back_out.at[ch],
                back_in.at[ch],
                device_id=dev,
                device_id_type=MESH_ID,
            ).start()

        back[pl.ds(me * own_width + ch * chunk, chunk)] = spatial[
            pl.ds(ch * chunk, chunk),
            pl.ds(pl.multiple_of(ilat * 32, 32), 32),
            pl.ds(pl.multiple_of(ilon * 128, 128), 128),
        ]

    for ch in range(chunks):
        wait_for(of_31(back), back_in.at[ch])

        @pl.loop(0, 32)
        def _(s):
            first = s * own_width + ch * chunk
            cells[pl.ds(pl.multiple_of(first * 32, 128), 128), :] = (
                back[pl.ds(first, chunk)].reshape(chunk * 32, 128).astype(F32)
            )

    def decode(r):
        for q in range(4):
            part = fields_t[r, :, q * 128 : (q + 1) * 128].astype(F32)
            part = part + cells[pl.ds(4 * r + q, width, stride=32), :]
            mixed[:, q * 128 : (q + 1) * 128] = part.astype(BF16)
        pa = mm(w_t[...], mixed[...]) + b[...]
        preact[r] = pa
        hidden = (pa / (1.0 + jnp.exp(-pa))).astype(BF16)
        pred[r] = mm(wo[...], hidden) + bo[...]

    @pl.loop(1, 9)
    def _(o):
        r = (im + o) % 8
        decode(r)

        @pl.when(o < 8)
        def _():
            pltpu.make_async_remote_copy(
                pred.at[r],
                pred_in.at[im],
                pred_out,
                pred_in_sem,
                device_id=at_member(r),
                device_id_type=MESH_ID,
            ).start()

    pred_in[im] = pred[im]
    wait_for(pred.at[pl.ds(0, 7)], pred_in_sem)
    first = pred_in[0]
    second = first * first
    for s in range(1, members):
        first = first + pred_in[s]
        second = second + pred_in[s] * pred_in[s]
    sums[im, 0] = first
    sums[im, 1] = second

    def sums_copy(index, m, sem_out, sem_in):
        return pltpu.make_async_remote_copy(
            sums.at[index],
            sums.at[index],
            sem_out,
            sem_in,
            device_id=at_member(m),
            device_id_type=MESH_ID,
        )

    for t in (1, 2, 3):
        sums_copy(im, (im + 2 * t) % 8, sums_out.at[t], sums_in.at[t]).start()
    sums_copy(im, partner, sums_out.at[0], sums_in.at[0]).start()

    def backward(r):
        mean = sums[r, 0] / members
        var = sums[r, 1] / members - mean * mean + variance_floor
        goal = jnp.concatenate(
            [targets[pl.ds(4 * r + q, 80, stride=32), :] for q in range(4)], axis=1
        )
        res = goal - mean
        inv = 1.0 / var
        loss = 0.5 * (jnp.log(var) + res * res * inv)
        for q in range(4):
            nll[pl.ds(4 * r + q, 80, stride=32), :] = loss[:, q * 128 : (q + 1) * 128]
        gp = (
            -res * inv / members
            + (inv - res * res * inv * inv) * (pred[r] - mean) / members
        ) / variables
        high = gp.astype(BF16)
        gpair[0:80, :] = high
        gpair[80:160, :] = (gp - high.astype(F32)).astype(BF16)
        gh = mm(wo_t[...], gpair[...])
        pa = preact[r]
        sg = 1.0 / (1.0 + jnp.exp(-pa))
        gpre = (gh * sg * (1.0 + pa * (1.0 - sg))).astype(BF16)
        gm = mm(w[...], gpre)
        for q in range(4):
            cells[pl.ds(4 * r + q, width, stride=32), :] = gm[:, q * 128 : (q + 1) * 128]

    @pl.loop(0, 8)
    def _(u):
        t = u // 2
        straight = (im + 8 - 2 * t) % 8
        passed = (partner + 8 - 2 * t) % 8
        even = u % 2 == 0

        @pl.when(jnp.logical_and(even, u > 0))
        def _():
            wait_for(sums.at[0], sums_in.at[t])
            sums_copy(straight, partner, fwd_out.at[t], fwd_in.at[t]).start()

        @pl.when(u == 1)
        def _():
            wait_for(sums.at[0], sums_in.at[0])

        @pl.when(jnp.logical_and(u % 2 == 1, u > 1))
        def _():
            wait_for(sums.at[0], fwd_in.at[t])

        backward(jnp.where(even, straight, passed))

    for ch in range(chunks):
        wait_for(of_31(block), out_sem.at[ch])
    fill_block()
    send_blocks(ggrid, gout_sem, gin_sem)

    gsum[...] = jnp.zeros_like(gsum)
    for ch in range(chunks):
        wait_for(of_31(block), gin_sem.at[ch])

        @pl.loop(ch * chunk, (ch + 1) * chunk)
        def _(c):
            own = lane == ilon * own_width + c
            g = to_spectral(ggrid[c])
            gr, gi = g[:, 0:256], g[:, 256:512]
            sr, si = spectrum[c, :, 0:256], spectrum[c, :, 256:512]
            g_re = jnp.sum(jnp.where(keep, gr * sr + gi * si, 0.0), axis=1, keepdims=True)
            g_im = jnp.sum(jnp.where(keep, gi * sr - gr * si, 0.0), axis=1, keepdims=True)
            gsum[0] = gsum[0] + jnp.where(own, g_re, 0.0)
            gsum[1] = gsum[1] + jnp.where(own, g_im, 0.0)

    @pl.loop(1, 4)
    def _(o):
        lo = (ilon + o) % 4
        pltpu.make_async_remote_copy(
            gsum.at[:, pl.ds(pl.multiple_of(lo * 64, 64), 64), :],
            gsum_in.at[ilon],
            grad_out,
            grad_in,
            device_id=(im, ilat, lo),
            device_id_type=MESH_ID,
        ).start()

    gsum_in[ilon] = gsum[:, pl.ds(pl.multiple_of(ilon * 64, 64), 64), :]
    wait_for(gsum_in.at[pl.ds(0, 3)], grad_in)
    grads[...] = gsum_in[0] + gsum_in[1] + gsum_in[2] + gsum_in[3]

    for ch in range(chunks):
        wait_for(of_31(back), back_out.at[ch])
        wait_for(of_31(block), gout_sem.at[ch])
    wait_for(pred.at[pl.ds(0, 7)], pred_out)
    for t in range(4):
        wait_for(sums.at[0], sums_out.at[t])
    for t in (1, 2, 3):
        wait_for(sums.at[0], fwd_out.at[t])
    wait_for(weights.at[:, pl.ds(0, 192), :], filt_out)
    wait_for(gsum_in.at[pl.ds(0, 3)], grad_out)


def on_device(fields, targets, filt_re, filt_im, w_in, b_in, w_out, b_out):
    lat_pad, lon_pad = tables()
    lat = jnp.asarray(lat_pad, BF16)
    lat_t = jnp.asarray(lat_pad.T.copy(), BF16)
    lon = jnp.asarray(lon_pad, BF16)
    lon_t = jnp.asarray(lon_pad.T.copy(), BF16)
    filters = jnp.pad(jnp.concatenate([filt_re, filt_im], axis=0), ((0, 0), (0, 4), (0, 80)))
    goal = jnp.pad(targets, ((0, 7), (0, 2), (0, 8))).reshape(80 * 32, 128)
    w = w_in[0]
    wo = jnp.pad(w_out[0], ((0, 7), (0, 0)))
    wo_t = jnp.concatenate([wo.T, wo.T], axis=1)
    vmem = pl.BlockSpec(memory_space=pltpu.VMEM)
    dma = pltpu.SemaphoreType.DMA
    nll, grads = pl.pallas_call(
        kernel,
        out_shape=(
            jax.ShapeDtypeStruct((80 * 32, 128), F32),
            jax.ShapeDtypeStruct((2, 64, 128), F32),
        ),
        in_specs=[vmem] * 13,
        out_specs=(vmem, vmem),
        scratch_shapes=[
            pltpu.VMEM((width * 32, 128), F32),
            pltpu.VMEM((8, width, 512), BF16),
            pltpu.VMEM((width, 32, 128), BF16),
            pltpu.VMEM((own_width, 256, 512), BF16),
            pltpu.VMEM((own_width, 256, 512), BF16),
            pltpu.VMEM((width, 32, 128), BF16),
            pltpu.VMEM((own_width, 256, 512), F32),
            pltpu.VMEM((8, width, 512), F32),
            pltpu.VMEM((8, 80, 512), F32),
            pltpu.VMEM((8, 80, 512), F32),
            pltpu.VMEM((8, 2, 80, 512), F32),
            pltpu.VMEM((own_width, 256, 512), BF16),
            pltpu.VMEM((2, 256, 128), F32),
            pltpu.VMEM((2, 256, 128), F32),
            pltpu.VMEM((4, 2, 64, 128), F32),
            pltpu.VMEM((width, 512), BF16),
            pltpu.VMEM((160, 512), BF16),
            dma((chunks,)),
            dma((chunks,)),
            dma((chunks,)),
            dma((chunks,)),
            dma((chunks,)),
            dma((chunks,)),
            dma,
            dma,
            dma((4,)),
            dma((4,)),
            dma((4,)),
            dma((4,)),
            dma,
            dma,
            dma,
            dma,
        ],
        compiler_params=pltpu.CompilerParams(
            collective_id=0, has_side_effects=True, vmem_limit_bytes=67043328
        ),
    )(
        fields[0], goal, filters, w, w.T, b_in[0][:, None], wo, wo_t,
        jnp.pad(b_out[0], (0, 7))[:, None], lat, lat_t, lon, lon_t,
    )
    nll = nll.reshape(80, 32, 128)[:variables, :own_rows, :own_columns]
    grads = grads[:, :60, :48]
    return nll, grads[0:1], grads[1:2]


def solution(mesh):
    placed = (
        P("member", "lat", "lon", None),
        P(None, "lat", "lon"),
        P("member", "lon", "lat"),
        P("member", "lon", "lat"),
        P("member", None, None),
        P("member", None),
        P("member", None, None),
        P("member", None),
    )
    return jax.shard_map(
        on_device,
        mesh=mesh,
        in_specs=placed,
        out_specs=(P(None, "lat", "lon"), P("member", "lon", "lat"), P("member", "lon", "lat")),
        check_vma=False,
    )
```

```python
import functools

import jax
import jax.numpy as jnp
import numpy as np
from jax import lax
from jax.experimental import pallas as pl
from jax.experimental.pallas import tpu as pltpu
from jax.sharding import PartitionSpec as P

MESH_ID = pl.DeviceIdType.MESH
F32 = jnp.float32
BF16 = jnp.bfloat16

rows, columns, width, variables, members = 240, 480, 384, 73, 8
own_rows, own_columns, own_width = 30, 120, 12
chunks = 3
chunk = own_width // chunks
variance_floor = 0.1


def tables():
    k = np.arange(rows, dtype=np.float64)[:, None]
    j = np.arange(rows, dtype=np.float64)[None, :]
    lat = np.where(k == 0, np.sqrt(1.0 / rows), np.sqrt(2.0 / rows)) * np.cos(
        np.pi * k * (j + 0.5) / rows
    )
    half = columns // 2
    place = np.arange(columns, dtype=np.int64)[:, None]
    order = np.arange(half, dtype=np.int64)[None, :]
    angle = 2.0 * np.pi * (place * order % columns).astype(np.float64) / columns
    scale = np.where(order == 0, np.sqrt(1.0 / columns), np.sqrt(2.0 / columns))
    kpad = (np.arange(rows) // 60) * 64 + np.arange(rows) % 60
    jpad = (np.arange(rows) // 30) * 32 + np.arange(rows) % 30
    lpad = (np.arange(columns) // 120) * 128 + np.arange(columns) % 120
    lat_pad = np.zeros((256, 256), np.float32)
    lat_pad[np.ix_(kpad, jpad)] = lat
    lon_pad = np.zeros((512, 512), np.float32)
    lon_pad[np.ix_(lpad, np.arange(half))] = scale * np.cos(angle)
    lon_pad[np.ix_(lpad, 256 + np.arange(half))] = -scale * np.sin(angle)
    return lat_pad, lon_pad


def mm(a, b):
    return jnp.dot(a, b, preferred_element_type=F32)


def wait_for(ref, sem):
    pltpu.make_async_copy(ref, ref, sem).wait()


def kernel(
    fields_hbm, targets_hbm, fre_hbm, fim_hbm, w_hbm, b_hbm, wo_hbm, bo_hbm,
    lat_hbm, lat_t_hbm, lon_hbm, lon_t_hbm,
    nll, grad_re, grad_im,
    fields, targets, fre, fim, w, b, wo, bo, lat, lat_t, lon, lon_t,
    goal, loss_rows, filters, square, w_t, b_col, wo_pad, wo_t, bo_col,
    cells, fields_t, block, grid, spatial, back, spectrum, preact, pred, pred_in, sums, ggrid,
    weights, gsum, gsum_in, mixed, gpair,
    load_sem, out_sem, in_sem, back_out, back_in, gout_sem, gin_sem, pred_out, pred_in_sem,
    sums_out, sums_in, fwd_out, fwd_in, filt_out, filt_in, grad_out, grad_in,
):
    im = lax.axis_index("member")
    ilat = lax.axis_index("lat")
    ilon = lax.axis_index("lon")
    me = ilat * 4 + ilon
    partner = (im // 2) * 2 + 1 - im % 2

    def peer(o):
        y, z = ilat % 4, (ilat // 4) * 4 + ilon
        y2, z2 = (y + o % 4) % 4, (z + o // 4) % 8
        la, lo = (z2 // 4) * 4 + y2, z2 % 4
        return (im, la, lo), la, lo

    def at_member(m):
        return (m, ilat, ilon)

    def load_fields(i):
        part = pl.ds(i * 6, 6)
        return pltpu.make_async_copy(fields_hbm.at[0, part], fields.at[part], load_sem.at[i])

    later = [
        pltpu.make_async_copy(src, dst, load_sem.at[5 + i])
        for i, (src, dst) in enumerate(
            [
                (fre_hbm, fre), (fim_hbm, fim), (lat_hbm, lat), (lon_hbm, lon),
                (lat_t_hbm, lat_t), (lon_t_hbm, lon_t), (w_hbm, w), (b_hbm, b),
                (wo_hbm, wo), (bo_hbm, bo), (targets_hbm, targets),
            ]
        )
    ]
    for i in range(5):
        load_fields(i).start()
    for copy in later:
        copy.start()

    barrier = pltpu.get_barrier_semaphore()

    @pl.loop(1, 32)
    def _(o):
        pl.semaphore_signal(barrier, 1, device_id=peer(o)[0], device_id_type=MESH_ID)

    @pl.loop(1, 8)
    def _(o):
        pl.semaphore_signal(
            barrier, 1, device_id=at_member((im + o) % 8), device_id_type=MESH_ID
        )

    def grid_part(c0, n, la, lo, half=None):
        start, size = (la * 32, 32) if half is None else (la * 32 + half * 16, 16)
        return (
            pl.ds(c0, n),
            pl.ds(pl.multiple_of(start, 16), size),
            pl.ds(pl.multiple_of(lo * 128, 128), 128),
        )

    def block_part(c0, n, la, lo, half=None):
        start, size = (0, 32) if half is None else (half * 16, 16)
        return (pl.ds((la * 4 + lo) * own_width + c0, n), pl.ds(start, size))

    def to_owners(target, c0, n, half, sem_out, sem_in):
        @pl.loop(1, 32)
        def _(o):
            dev, la, lo = peer(o)
            pltpu.make_async_remote_copy(
                block.at[block_part(c0, n, la, lo, half)],
                target.at[grid_part(c0, n, ilat, ilon, half)],
                sem_out,
                sem_in,
                device_id=dev,
                device_id_type=MESH_ID,
            ).start()

        target[grid_part(c0, n, ilat, ilon, half)] = block[block_part(c0, n, ilat, ilon, half)]

    def to_cells(c0, n, half, sem_out, sem_in):
        @pl.loop(1, 32)
        def _(o):
            dev, la, lo = peer(o)
            pltpu.make_async_remote_copy(
                spatial.at[grid_part(c0, n, la, lo, half)],
                back.at[block_part(c0, n, ilat, ilon, half)],
                sem_out,
                sem_in,
                device_id=dev,
                device_id_type=MESH_ID,
            ).start()

        back[block_part(c0, n, ilat, ilon, half)] = spatial[grid_part(c0, n, ilat, ilon, half)]

    def wait_31(n, half, sem):
        size = 32 if half is None else 16
        wait_for(block.at[pl.ds(0, 31 * n), pl.ds(0, size)], sem)

    def turn(j, q):
        x = fields[j].astype(F32)
        x = jnp.concatenate([x, jnp.zeros((8, width), F32)], axis=0).T
        cells[pl.ds(j, width, stride=32), :] = x
        fields_t[j // 4, :, q * 128 : (q + 1) * 128] = x.astype(BF16)

    def fill_block(half):
        @pl.loop(0, width // 8)
        def _(i):
            for c in range(8):
                part = cells[pl.ds(pl.multiple_of(i * 256 + c * 32 + half * 16, 16), 16), :]
                block[i * 8 + c, pl.ds(half * 16, 16), :] = part.astype(BF16)

    for i in range(3):
        load_fields(i).wait()

    @pl.loop(0, 4)
    def _(u):
        for q in range(4):
            turn(u * 4 + q, q)

    fill_block(0)
    pl.semaphore_wait(barrier, 31 + 7)
    to_owners(grid, 0, chunk, 0, out_sem.at[0], in_sem.at[0])

    for i in range(3, 5):
        load_fields(i).wait()

    @pl.loop(4, 7)
    def _(u):
        for q in range(4):
            turn(u * 4 + q, q)

    turn(28, 0)
    turn(29, 1)
    for j in (30, 31):
        cells[pl.ds(j, width, stride=32), :] = jnp.zeros((width, 128), F32)
    fields_t[7, :, 256:512] = jnp.zeros((width, 256), BF16)
    fill_block(1)
    to_owners(grid, 0, chunk, 1, out_sem.at[1], in_sem.at[1])
    for ch in range(1, chunks):
        to_owners(grid, ch * chunk, chunk, None, out_sem.at[ch + 1], in_sem.at[ch + 1])

    for copy in later:
        copy.wait()
    for n, part in enumerate((fre, fim)):
        square[...] = jnp.zeros_like(square)
        square[0:48, 0:60] = part[0]
        filters[n] = square[...].T[0:64]

    @pl.loop(1, 4)
    def _(o):
        pltpu.make_async_remote_copy(
            filters,
            weights.at[:, pl.ds(pl.multiple_of(ilon * 64, 64), 64), :],
            filt_out,
            filt_in,
            device_id=(im, ilat, (ilon + o) % 4),
            device_id_type=MESH_ID,
        ).start()

    weights[:, pl.ds(pl.multiple_of(ilon * 64, 64), 64), :] = filters[...]

    w_t[...] = w[0].astype(F32).T.astype(BF16)
    b_col[...] = jnp.broadcast_to(b[...], (128, width)).T
    wo_pad[...] = jnp.zeros_like(wo_pad)
    wo_pad[0:variables, :] = wo[0].astype(F32)
    turned = wo_pad[...].T.astype(BF16)
    wo_t[:, 0:128] = turned
    wo_t[:, 128:256] = turned
    bo_col[...] = jnp.zeros_like(bo_col)
    bo_col[0:1, 0:variables] = bo[...]
    bo_col[...] = jnp.broadcast_to(bo_col[0:1, :], (128, 128)).T
    goal[...] = jnp.zeros_like(goal)

    @pl.loop(0, variables)
    def _(v):
        goal[pl.ds(pl.multiple_of(v * 32, 32), own_rows), 0:own_columns] = targets[v]

    gpair[...] = jnp.zeros_like(gpair)
    gsum[...] = jnp.zeros_like(gsum)
    wait_for(weights.at[:, pl.ds(0, 192), :], filt_in)

    lane = lax.broadcasted_iota(jnp.int32, (256, 128), 1)
    k_row = lax.broadcasted_iota(jnp.int32, (256, 256), 0)
    keep = (k_row // 64) * 60 + k_row % 64 >= lax.broadcasted_iota(jnp.int32, (256, 256), 1)

    def to_spectral(x):
        return mm(mm(lat[...], x).astype(BF16), lon[...])

    for ch in range(chunks):
        if ch == 0:
            wait_31(chunk, 0, in_sem.at[0])
            wait_31(chunk, 1, in_sem.at[1])
        else:
            wait_31(chunk, None, in_sem.at[ch + 1])

        @pl.loop(ch * chunk, (ch + 1) * chunk)
        def _(c):
            own = lane == ilon * own_width + c
            wr = jnp.sum(jnp.where(own, weights[0], 0.0), axis=1, keepdims=True)
            wi = jnp.sum(jnp.where(own, weights[1], 0.0), axis=1, keepdims=True)
            spectrum[c] = to_spectral(grid[c])
            sr, si = spectrum[c, :, 0:256], spectrum[c, :, 256:512]
            fr = jnp.where(keep, wr * sr - wi * si, 0.0).astype(BF16)
            fi = jnp.where(keep, wr * si + wi * sr, 0.0).astype(BF16)
            lon_back = mm(jnp.concatenate([fr, fi], axis=1), lon_t[...]).astype(BF16)
            spatial[c] = mm(lat_t[...], lon_back).astype(BF16)

        if ch < chunks - 1:
            to_cells(ch * chunk, chunk, None, back_out.at[ch], back_in.at[ch])
        else:
            to_cells(ch * chunk, chunk, 0, back_out.at[ch], back_in.at[ch])
            to_cells(ch * chunk, chunk, 1, back_out.at[ch + 1], back_in.at[ch + 1])

    def unpack(ch, half):
        @pl.loop(0, 32)
        def _(s):
            first = s * own_width + ch * chunk
            for c in range(chunk):
                rows_at = pl.multiple_of((first + c) * 32 + half * 16, 16)
                part = back[first + c, pl.ds(half * 16, 16), :]
                cells[pl.ds(rows_at, 16), :] = part.astype(F32)

    def decode(half, i):
        u = half * 4 + i
        for q in range(4):
            part = fields_t[u, :, q * 128 : (q + 1) * 128].astype(F32)
            part = part + cells[pl.ds(4 * u + q, width, stride=32), :]
            mixed[:, q * 128 : (q + 1) * 128] = part.astype(BF16)
        bias = b_col[...]
        pa = mm(w_t[...], mixed[...]) + jnp.concatenate([bias] * 4, axis=1)
        preact[u] = pa
        hidden = (pa / (1.0 + jnp.exp(-pa))).astype(BF16)
        bias = bo_col[0:80, :]
        out = mm(wo_pad[0:80, :].astype(BF16), hidden) + jnp.concatenate([bias] * 4, axis=1)
        pred[half, 2 * i] = out[:, 0:256]
        pred[half, 2 * i + 1] = out[:, 256:512]

    def decode_half(half):
        @pl.loop(0, 4)
        def _(o):
            i = (im // 2 + 1 + o) % 4
            decode(half, i)
            for e in range(2):
                r = 2 * i + e

                @pl.when(r != im)
                def _():
                    pltpu.make_async_remote_copy(
                        pred.at[half, r],
                        pred_in.at[half, im],
                        pred_out.at[half],
                        pred_in_sem.at[half],
                        device_id=at_member(r),
                        device_id_type=MESH_ID,
                    ).start()

    def sums_copy(half, index, m, sem_out, sem_in):
        return pltpu.make_async_remote_copy(
            sums.at[half, index],
            sums.at[half, index],
            sem_out,
            sem_in,
            device_id=at_member(m),
            device_id_type=MESH_ID,
        )

    def sum_half(half):
        pred_in[half, im] = pred[half, im]
        wait_for(pred.at[half, pl.ds(0, 7)], pred_in_sem.at[half])
        first = pred_in[half, 0]
        second = first * first
        for s in range(1, members):
            one = pred_in[half, s]
            first = first + one
            second = second + one * one
        sums[half, im, 0] = first
        sums[half, im, 1] = second
        for t in (1, 2, 3):
            sums_copy(
                half, im, (im + 2 * t) % 8, sums_out.at[half, t], sums_in.at[half, t]
            ).start()
        sums_copy(half, im, partner, sums_out.at[half, 0], sums_in.at[half, 0]).start()

    def backward(half, i):
        u = half * 4 + i
        mean, var = [
            jnp.concatenate([sums[half, 2 * i, n], sums[half, 2 * i + 1, n]], axis=1) / members
            for n in range(2)
        ]
        own_pred = jnp.concatenate([pred[half, 2 * i], pred[half, 2 * i + 1]], axis=1)
        var = var - mean * mean + variance_floor
        want = jnp.concatenate(
            [goal[pl.ds(4 * u + q, 80, stride=32), :] for q in range(4)], axis=1
        )
        res = want - mean
        inv = 1.0 / var
        loss = 0.5 * (jnp.log(var) + res * res * inv)
        for q in range(4):
            loss_rows[pl.ds(4 * u + q, 80, stride=32), :] = loss[:, q * 128 : (q + 1) * 128]
        gp = (
            -res * inv / members
            + (inv - res * res * inv * inv) * (own_pred - mean) / members
        ) / variables
        high = gp.astype(BF16)
        gpair[0:80, :] = high
        gpair[128:208, :] = (gp - high.astype(F32)).astype(BF16)
        gh = mm(wo_t[...], gpair[...])
        pa = preact[u]
        sg = 1.0 / (1.0 + jnp.exp(-pa))
        gpre = (gh * sg * (1.0 + pa * (1.0 - sg))).astype(BF16)
        gm = mm(w[0], gpre)
        for q in range(4):
            cells[pl.ds(4 * u + q, width, stride=32), :] = gm[:, q * 128 : (q + 1) * 128]

    def backward_half(half):
        wait_for(sums.at[half, 0], sums_in.at[half, 0])
        backward(half, im // 2)
        for t in (1, 2, 3):
            wait_for(sums.at[half, 0], sums_in.at[half, t])
            sums_copy(
                half, (im + 8 - 2 * t) % 8, partner, fwd_out.at[half, t], fwd_in.at[half, t]
            ).start()

        @pl.loop(1, 4)
        def _(t):
            wait_for(sums.at[half, 0], fwd_in.at[half, t])
            backward(half, (im // 2 + 4 - t) % 4)

    for ch in range(chunks):
        wait_31(chunk, None if ch < chunks - 1 else 0, back_in.at[ch])
        unpack(ch, 0)
    decode_half(0)
    for ch in range(chunks - 1):
        unpack(ch, 1)
    sum_half(0)
    wait_31(chunk, 1, back_in.at[chunks])
    unpack(chunks - 1, 1)
    decode_half(1)
    wait_31(chunk, 0, out_sem.at[0])
    wait_31(chunk, 1, out_sem.at[1])
    for ch in range(1, chunks):
        wait_31(chunk, None, out_sem.at[ch + 1])
    backward_half(0)
    fill_block(0)
    to_owners(ggrid, 0, own_width, 0, gout_sem.at[chunks], gin_sem.at[chunks])
    sum_half(1)
    backward_half(1)
    fill_block(1)
    for ch in range(chunks):
        to_owners(ggrid, ch * chunk, chunk, 1, gout_sem.at[ch], gin_sem.at[ch])

    @pl.loop(0, variables)
    def _(v):
        nll[v] = loss_rows[pl.ds(pl.multiple_of(v * 32, 32), own_rows), 0:own_columns]

    wait_31(own_width, 0, gin_sem.at[chunks])
    for ch in range(chunks):
        wait_31(chunk, 1, gin_sem.at[ch])

        @pl.loop(ch * chunk, (ch + 1) * chunk)
        def _(c):
            own = lane == ilon * own_width + c
            g = to_spectral(ggrid[c])
            gr, gi = g[:, 0:256], g[:, 256:512]
            sr, si = spectrum[c, :, 0:256], spectrum[c, :, 256:512]
            g_re = jnp.sum(jnp.where(keep, gr * sr + gi * si, 0.0), axis=1, keepdims=True)
            g_im = jnp.sum(jnp.where(keep, gi * sr - gr * si, 0.0), axis=1, keepdims=True)
            gsum[0] = gsum[0] + jnp.where(own, g_re, 0.0)
            gsum[1] = gsum[1] + jnp.where(own, g_im, 0.0)

    @pl.loop(1, 4)
    def _(o):
        lo = (ilon + o) % 4
        pltpu.make_async_remote_copy(
            gsum.at[:, pl.ds(pl.multiple_of(lo * 64, 64), 64), :],
            gsum_in.at[ilon],
            grad_out,
            grad_in,
            device_id=(im, ilat, lo),
            device_id_type=MESH_ID,
        ).start()

    gsum_in[ilon] = gsum[:, pl.ds(pl.multiple_of(ilon * 64, 64), 64), :]
    wait_for(gsum_in.at[pl.ds(0, 3)], grad_in)
    total = gsum_in[0] + gsum_in[1] + gsum_in[2] + gsum_in[3]
    for n, part in enumerate((grad_re, grad_im)):
        square[0:64] = total[n]
        part[0] = square[...].T[0:48, 0:60]

    for ch in range(chunks - 1):
        wait_31(chunk, None, back_out.at[ch])
    wait_31(chunk, 0, back_out.at[chunks - 1])
    wait_31(chunk, 1, back_out.at[chunks])
    wait_31(own_width, 0, gout_sem.at[chunks])
    for ch in range(chunks):
        wait_31(chunk, 1, gout_sem.at[ch])
    for half in range(2):
        wait_for(pred.at[half, pl.ds(0, 7)], pred_out.at[half])
        for t in range(4):
            wait_for(sums.at[half, 0], sums_out.at[half, t])
        for t in (1, 2, 3):
            wait_for(sums.at[half, 0], fwd_out.at[half, t])
    wait_for(weights.at[:, pl.ds(0, 192), :], filt_out)
    wait_for(gsum_in.at[pl.ds(0, 3)], grad_out)


def on_device(fields, targets, filt_re, filt_im, w_in, b_in, w_out, b_out):
    lat_pad, lon_pad = tables()
    lat = jnp.asarray(lat_pad, BF16)
    lat_t = jnp.asarray(lat_pad.T.copy(), BF16)
    lon = jnp.asarray(lon_pad, BF16)
    lon_t = jnp.asarray(lon_pad.T.copy(), BF16)
    anywhere = pl.BlockSpec(memory_space=pl.ANY)
    vmem = pl.BlockSpec(memory_space=pltpu.VMEM)
    dma = pltpu.SemaphoreType.DMA
    filt_re, filt_im = jnp.swapaxes(filt_re, 1, 2), jnp.swapaxes(filt_im, 1, 2)
    nll, grad_re, grad_im = pl.pallas_call(
        kernel,
        out_shape=(
            jax.ShapeDtypeStruct(targets.shape, F32),
            jax.ShapeDtypeStruct(filt_re.shape, F32),
            jax.ShapeDtypeStruct(filt_re.shape, F32),
        ),
        in_specs=[anywhere] * 12,
        out_specs=(vmem, vmem, vmem),
        scratch_shapes=[
            pltpu.VMEM(fields.shape[1:], BF16),
            pltpu.VMEM(targets.shape, F32),
            pltpu.VMEM(filt_re.shape, F32),
            pltpu.VMEM(filt_im.shape, F32),
            pltpu.VMEM(w_in.shape, BF16),
            pltpu.VMEM(b_in.shape, F32),
            pltpu.VMEM(w_out.shape, BF16),
            pltpu.VMEM(b_out.shape, F32),
            pltpu.VMEM((256, 256), BF16),
            pltpu.VMEM((256, 256), BF16),
            pltpu.VMEM((512, 512), BF16),
            pltpu.VMEM((512, 512), BF16),
            pltpu.VMEM((80 * 32, 128), F32),
            pltpu.VMEM((80 * 32, 128), F32),
            pltpu.VMEM((2, 64, 128), F32),
            pltpu.VMEM((128, 128), F32),
            pltpu.VMEM((width, width), BF16),
            pltpu.VMEM((width, 128), F32),
            pltpu.VMEM((128, width), F32),
            pltpu.VMEM((width, 256), BF16),
            pltpu.VMEM((128, 128), F32),
            pltpu.VMEM((width * 32, 128), F32),
            pltpu.VMEM((8, width, 512), BF16),
            pltpu.VMEM((width, 32, 128), BF16),
            pltpu.VMEM((own_width, 256, 512), BF16),
            pltpu.VMEM((own_width, 256, 512), BF16),
            pltpu.VMEM((width, 32, 128), BF16),
            pltpu.VMEM((own_width, 256, 512), F32),
            pltpu.VMEM((8, width, 512), F32),
            pltpu.VMEM((2, 8, 80, 256), F32),
            pltpu.VMEM((2, 8, 80, 256), F32),
            pltpu.VMEM((2, 8, 2, 80, 256), F32),
            pltpu.VMEM((own_width, 256, 512), BF16),
            pltpu.VMEM((2, 256, 128), F32),
            pltpu.VMEM((2, 256, 128), F32),
            pltpu.VMEM((4, 2, 64, 128), F32),
            pltpu.VMEM((width, 512), BF16),
            pltpu.VMEM((256, 512), BF16),
            dma((16,)),
            dma((chunks + 1,)),
            dma((chunks + 1,)),
            dma((chunks + 1,)),
            dma((chunks + 1,)),
            dma((chunks + 1,)),
            dma((chunks + 1,)),
            dma((2,)),
            dma((2,)),
            dma((2, 4)),
            dma((2, 4)),
            dma((2, 4)),
            dma((2, 4)),
            dma,
            dma,
            dma,
            dma,
        ],
        compiler_params=pltpu.CompilerParams(
            collective_id=0, has_side_effects=True, vmem_limit_bytes=67043328
        ),
    )(fields, targets, filt_re, filt_im, w_in, b_in, w_out, b_out, lat, lat_t, lon, lon_t)
    return nll, jnp.swapaxes(grad_re, 1, 2), jnp.swapaxes(grad_im, 1, 2)


def solution(mesh):
    placed = (
        P("member", "lat", "lon", None),
        P(None, "lat", "lon"),
        P("member", "lon", "lat"),
        P("member", "lon", "lat"),
        P("member", None, None),
        P("member", None),
        P("member", None, None),
        P("member", None),
    )
    return jax.shard_map(
        on_device,
        mesh=mesh,
        in_specs=placed,
        out_specs=(P(None, "lat", "lon"), P("member", "lon", "lat"), P("member", "lon", "lat")),
        check_vma=False,
    )
```

```python
import functools

import jax
import jax.numpy as jnp
import numpy as np
from jax import lax
from jax.experimental import pallas as pl
from jax.experimental.pallas import tpu as pltpu
from jax.sharding import PartitionSpec as P

MESH_ID = pl.DeviceIdType.MESH
F32 = jnp.float32
BF16 = jnp.bfloat16

rows, columns, width, variables, members = 240, 480, 384, 73, 8
own_rows, own_columns, own_width = 30, 120, 12
low = 14
chunks = 3
chunk = own_width // chunks
variance_floor = 0.1


def tables():
    k = np.arange(rows, dtype=np.float64)[:, None]
    j = np.arange(rows, dtype=np.float64)[None, :]
    lat = np.where(k == 0, np.sqrt(1.0 / rows), np.sqrt(2.0 / rows)) * np.cos(
        np.pi * k * (j + 0.5) / rows
    )
    half = columns // 2
    place = np.arange(columns, dtype=np.int64)[:, None]
    order = np.arange(half, dtype=np.int64)[None, :]
    angle = 2.0 * np.pi * (place * order % columns).astype(np.float64) / columns
    scale = np.where(order == 0, np.sqrt(1.0 / columns), np.sqrt(2.0 / columns))
    kpad = (np.arange(rows) // 60) * 64 + np.arange(rows) % 60
    part, inside = np.arange(rows) // 30, np.arange(rows) % 30
    jpad = np.where(inside < 16, part * 16 + inside, 128 + part * 16 + inside - 16)
    lpad = (np.arange(columns) // 120) * 128 + np.arange(columns) % 120
    lat_pad = np.zeros((256, 256), np.float32)
    lat_pad[np.ix_(kpad, jpad)] = lat
    lon_pad = np.zeros((512, 512), np.float32)
    lon_pad[np.ix_(lpad, np.arange(half))] = scale * np.cos(angle)
    lon_pad[np.ix_(lpad, 256 + np.arange(half))] = -scale * np.sin(angle)
    return lat_pad, lon_pad


def mm(a, b):
    return jnp.dot(a, b, preferred_element_type=F32)


def wait_for(ref, sem):
    pltpu.make_async_copy(ref, ref, sem).wait()


def kernel(
    fields_hbm, targets_hbm, fre_hbm, fim_hbm, w_hbm, b_hbm, wo_hbm, bo_hbm,
    lat_hbm, lat_t_hbm, lon_hbm, lon_t_hbm,
    nll, grad_re, grad_im,
    fields, targets, fre, fim, w, b, wo, bo, lat, lat_t, lon, lon_t,
    goal, loss_rows, filters, square, w_t, b_col, wo_pad, wo_t, bo_col,
    cells, fields_t, block, block_low, grid, grid_low, spatial, spatial_low, back, back_low,
    spectrum, preact, pred, pred_in, sums, ggrid, ggrid_low, line, nll_all,
    weights, gsum, gsum_in, mixed, gpair,
    load_sem, nll_sem, out_sem, in_sem, back_out, back_in, gout_sem, gin_sem, pred_out, pred_in_sem,
    sums_out, sums_in, fwd_out, fwd_in, filt_out, filt_in, grad_out, grad_in,
):
    im = lax.axis_index("member")
    ilat = lax.axis_index("lat")
    ilon = lax.axis_index("lon")
    me = ilat * 4 + ilon
    partner = (im // 2) * 2 + 1 - im % 2

    def peer(o):
        y, z = ilat % 4, (ilat // 4) * 4 + ilon
        y2, z2 = (y + o % 4) % 4, (z + o // 4) % 8
        la, lo = (z2 // 4) * 4 + y2, z2 % 4
        return (im, la, lo), la, lo

    def at_member(m):
        return (m, ilat, ilon)

    def load_fields(i):
        part = pl.ds(i * 6, 6)
        return pltpu.make_async_copy(fields_hbm.at[0, part], fields.at[part], load_sem.at[i])

    later = [
        pltpu.make_async_copy(src, dst, load_sem.at[5 + i])
        for i, (src, dst) in enumerate(
            [
                (fre_hbm, fre), (fim_hbm, fim), (lat_hbm, lat), (lon_hbm, lon),
                (lat_t_hbm, lat_t), (lon_t_hbm, lon_t), (w_hbm, w), (b_hbm, b),
                (wo_hbm, wo), (bo_hbm, bo), (targets_hbm, targets),
            ]
        )
    ]
    for i in range(5):
        load_fields(i).start()
    for copy in later:
        copy.start()

    barrier = pltpu.get_barrier_semaphore()

    @pl.loop(1, 32)
    def _(o):
        pl.semaphore_signal(barrier, 1, device_id=peer(o)[0], device_id_type=MESH_ID)

    @pl.loop(1, 8)
    def _(o):
        pl.semaphore_signal(
            barrier, 1, device_id=at_member((im + o) % 8), device_id_type=MESH_ID
        )

    def grid_part(c0, n, la, lo):
        return (
            pl.ds(c0, n),
            pl.ds(pl.multiple_of(la * 16, 16), 16),
            pl.ds(pl.multiple_of(lo * 128, 128), 128),
        )

    def block_part(c0, n, la, lo):
        return (pl.ds((la * 4 + lo) * own_width + c0, n),)

    def low_part(c0, n, la, lo):
        return (la * 4 + lo, pl.ds(c0 * low, n * low))

    def exchange(src, src_part, dst, dst_part, c0, n, sem_out, sem_in):
        @pl.loop(1, 32)
        def _(o):
            dev, la, lo = peer(o)
            pltpu.make_async_remote_copy(
                src.at[src_part(c0, n, la, lo)],
                dst.at[dst_part(c0, n, ilat, ilon)],
                sem_out,
                sem_in,
                device_id=dev,
                device_id_type=MESH_ID,
            ).start()

        dst[dst_part(c0, n, ilat, ilon)] = src[src_part(c0, n, ilat, ilon)]

    def to_owners(target, c0, n, sem_out, sem_in):
        exchange(block, block_part, target, grid_part, c0, n, sem_out, sem_in)

    def low_to_owners(target, c0, n, sem_out, sem_in):
        exchange(block_low, low_part, target, low_part, c0, n, sem_out, sem_in)

    def wait_31(n, sem):
        wait_for(block.at[pl.ds(0, 31 * n)], sem)

    def wait_low(n, sem):
        wait_for(block_low.at[pl.ds(0, 31), pl.ds(0, n * low)], sem)

    def turn(j, q):
        x = fields[j].astype(F32)
        x = jnp.concatenate([x, jnp.zeros((8, width), F32)], axis=0).T
        cells[pl.ds(j, width, stride=32), :] = x
        fields_t[j // 4, :, q * 128 : (q + 1) * 128] = x.astype(BF16)

    def fill_block():
        @pl.loop(0, width // 8)
        def _(i):
            for c in range(8):
                part = cells[pl.ds(pl.multiple_of(i * 256 + c * 32, 32), 16), :]
                block[i * 8 + c] = part.astype(BF16)

    def fill_low():
        @pl.loop(0, 16)
        def _(i):
            for e in range(2):
                d = i * 2 + e
                for c in range(own_width):
                    first = pl.multiple_of((d * own_width + c) * 32 + 16, 16)
                    line[e, pl.ds(c * low, 16), :] = cells[pl.ds(first, 16), :]
                block_low[d] = line[e, 0 : own_width * low, :].astype(BF16)

    def spread_low(src, target, ch):
        @pl.loop(0, 8)
        def _(la):
            for lo in range(4):
                part = src[la * 4 + lo, pl.ds(ch * chunk * low, chunk * low)]
                line[lo, 0 : chunk * low, :] = part.astype(F32)
                for c in range(chunk):
                    target[
                        ch * chunk + c,
                        pl.ds(pl.multiple_of(128 + la * 16, 16), 16),
                        lo * 128 : (lo + 1) * 128,
                    ] = line[lo, pl.ds(c * low, 16), :].astype(BF16)

    line[...] = jnp.zeros_like(line)

    for i in range(3):
        load_fields(i).wait()

    @pl.loop(0, 4)
    def _(u):
        for q in range(4):
            turn(u * 4 + q, q)

    fill_block()

    for copy in later[:2]:
        copy.wait()
    for n, part in enumerate((fre, fim)):
        square[...] = jnp.zeros_like(square)
        square[0:48, 0:60] = part[0]
        filters[n] = square[...].T[0:64]

    pl.semaphore_wait(barrier, 31 + 7)

    @pl.loop(1, 4)
    def _(o):
        pltpu.make_async_remote_copy(
            filters,
            weights.at[:, pl.ds(pl.multiple_of(ilon * 64, 64), 64), :],
            filt_out,
            filt_in,
            device_id=(im, ilat, (ilon + o) % 4),
            device_id_type=MESH_ID,
        ).start()

    weights[:, pl.ds(pl.multiple_of(ilon * 64, 64), 64), :] = filters[...]

    to_owners(grid, 0, chunk, out_sem.at[0], in_sem.at[0])

    for i in range(3, 5):
        load_fields(i).wait()

    @pl.loop(4, 7)
    def _(u):
        for q in range(4):
            turn(u * 4 + q, q)

    turn(28, 0)
    turn(29, 1)
    for j in (30, 31):
        cells[pl.ds(j, width, stride=32), :] = jnp.zeros((width, 128), F32)
    fields_t[7, :, 256:512] = jnp.zeros((width, 256), BF16)
    fill_low()
    for ch in range(chunks):
        if ch > 0:
            to_owners(grid, ch * chunk, chunk, out_sem.at[ch], in_sem.at[ch])
        low_to_owners(
            grid_low, ch * chunk, chunk, out_sem.at[chunks + ch], in_sem.at[chunks + ch]
        )

    for copy in later[2:]:
        copy.wait()

    w_t[...] = w[0].astype(F32).T.astype(BF16)
    b_col[...] = jnp.broadcast_to(b[...], (128, width)).T
    wo_pad[...] = jnp.zeros_like(wo_pad)
    wo_pad[0:variables, :] = wo[0].astype(F32)
    turned = wo_pad[...].T.astype(BF16)
    wo_t[:, 0:128] = turned
    wo_t[:, 128:256] = turned
    bo_col[...] = jnp.zeros_like(bo_col)
    bo_col[0:1, 0:variables] = bo[...]
    bo_col[...] = jnp.broadcast_to(bo_col[0:1, :], (128, 128)).T
    goal[...] = jnp.zeros_like(goal)

    @pl.loop(0, variables)
    def _(v):
        goal[pl.ds(pl.multiple_of(v * 32, 32), own_rows), 0:own_columns] = targets[v]

    gpair[...] = jnp.zeros_like(gpair)
    gsum[...] = jnp.zeros_like(gsum)
    wait_for(weights.at[:, pl.ds(0, 192), :], filt_in)

    lane = lax.broadcasted_iota(jnp.int32, (256, 128), 1)
    k_row = lax.broadcasted_iota(jnp.int32, (256, 256), 0)
    keep = (k_row // 64) * 60 + k_row % 64 >= lax.broadcasted_iota(jnp.int32, (256, 256), 1)

    def to_spectral(x):
        return mm(mm(lat[...], x).astype(BF16), lon[...])

    for ch in range(chunks):
        wait_31(chunk, in_sem.at[ch])
        wait_low(chunk, in_sem.at[chunks + ch])
        spread_low(grid_low, grid, ch)

        @pl.loop(ch * chunk, (ch + 1) * chunk)
        def _(c):
            own = lane == ilon * own_width + c
            wr = jnp.sum(jnp.where(own, weights[0], 0.0), axis=1, keepdims=True)
            wi = jnp.sum(jnp.where(own, weights[1], 0.0), axis=1, keepdims=True)
            spectrum[c] = to_spectral(grid[c])
            sr, si = spectrum[c, :, 0:256], spectrum[c, :, 256:512]
            fr = jnp.where(keep, wr * sr - wi * si, 0.0).astype(BF16)
            fi = jnp.where(keep, wr * si + wi * sr, 0.0).astype(BF16)
            lon_back = mm(jnp.concatenate([fr, fi], axis=1), lon_t[...]).astype(BF16)
            spatial[c] = mm(lat_t[0:128, :], lon_back).astype(BF16)
            rest = mm(lat_t[128:256, :], lon_back)
            for la in range(8):
                for lo in range(4):
                    cells[pl.ds((la * 4 + lo) * 176 + c * low, 16), :] = rest[
                        la * 16 : la * 16 + 16, lo * 128 : lo * 128 + 128
                    ]

        exchange(
            spatial, grid_part, back, block_part, ch * chunk, chunk, back_out.at[ch], back_in.at[ch]
        )

    @pl.loop(0, 32)
    def _(d):
        part = cells[pl.ds(pl.multiple_of(d * 176, 16), own_width * low), :]
        spatial_low[d] = part.astype(BF16)

    exchange(
        spatial_low, low_part, back_low, low_part, 0, own_width,
        back_out.at[chunks], back_in.at[chunks],
    )

    def unpack(ch):
        @pl.loop(0, 32)
        def _(s):
            first = s * own_width + ch * chunk
            for c in range(chunk):
                cells[pl.ds(pl.multiple_of((first + c) * 32, 32), 16), :] = back[first + c].astype(F32)

    def unpack_low():
        @pl.loop(0, 16)
        def _(i):
            for e in range(2):
                s = i * 2 + e
                line[e, 0 : own_width * low, :] = back_low[s].astype(F32)
                for c in range(own_width):
                    first = pl.multiple_of((s * own_width + c) * 32 + 16, 16)
                    cells[pl.ds(first, 16), :] = line[e, pl.ds(c * low, 16), :]

    def decode(half, i):
        u = half * 4 + i
        for q in range(4):
            part = fields_t[u, :, q * 128 : (q + 1) * 128].astype(F32)
            part = part + cells[pl.ds(4 * u + q, width, stride=32), :]
            mixed[:, q * 128 : (q + 1) * 128] = part.astype(BF16)
        bias = b_col[...]
        pa = mm(w_t[...], mixed[...]) + jnp.concatenate([bias] * 4, axis=1)
        preact[u] = pa
        hidden = (pa / (1.0 + jnp.exp(-pa))).astype(BF16)
        bias = bo_col[0:80, :]
        out = mm(wo_pad[0:80, :].astype(BF16), hidden) + jnp.concatenate([bias] * 4, axis=1)
        pred[half, 2 * i] = out[:, 0:256]
        pred[half, 2 * i + 1] = out[:, 256:512]

    def decode_half(half):
        @pl.loop(0, 4)
        def _(o):
            i = (im // 2 + 1 + o) % 4
            decode(half, i)
            for e in range(2):
                r = 2 * i + e

                @pl.when(r != im)
                def _():
                    pltpu.make_async_remote_copy(
                        pred.at[half, r],
                        pred_in.at[half, im],
                        pred_out.at[half],
                        pred_in_sem.at[half],
                        device_id=at_member(r),
                        device_id_type=MESH_ID,
                    ).start()

    def sums_copy(half, index, m, sem_out, sem_in):
        return pltpu.make_async_remote_copy(
            sums.at[half, index],
            sums.at[half, index],
            sem_out,
            sem_in,
            device_id=at_member(m),
            device_id_type=MESH_ID,
        )

    def sum_half(half):
        pred_in[half, im] = pred[half, im]
        wait_for(pred.at[half, pl.ds(0, 7)], pred_in_sem.at[half])
        first = pred_in[half, 0]
        second = first * first
        for s in range(1, members):
            one = pred_in[half, s]
            first = first + one
            second = second + one * one
        sums[half, im, 0] = first
        sums[half, im, 1] = second
        for t in (1, 2, 3):
            sums_copy(
                half, im, (im + 2 * t) % 8, sums_out.at[half, t], sums_in.at[half, t]
            ).start()
        sums_copy(half, im, partner, sums_out.at[half, 0], sums_in.at[half, 0]).start()

    def backward(half, i):
        u = half * 4 + i
        mean, var = [
            jnp.concatenate([sums[half, 2 * i, n], sums[half, 2 * i + 1, n]], axis=1) / members
            for n in range(2)
        ]
        own_pred = jnp.concatenate([pred[half, 2 * i], pred[half, 2 * i + 1]], axis=1)
        var = var - mean * mean + variance_floor
        want = jnp.concatenate(
            [goal[pl.ds(4 * u + q, 80, stride=32), :] for q in range(4)], axis=1
        )
        res = want - mean
        inv = 1.0 / var
        loss = 0.5 * (jnp.log(var) + res * res * inv)
        for q in range(4):
            loss_rows[pl.ds(4 * u + q, 80, stride=32), :] = loss[:, q * 128 : (q + 1) * 128]
        gp = (
            -res * inv / members
            + (inv - res * res * inv * inv) * (own_pred - mean) / members
        ) / variables
        high = gp.astype(BF16)
        gpair[0:80, :] = high
        gpair[128:208, :] = (gp - high.astype(F32)).astype(BF16)
        gh = mm(wo_t[...], gpair[...])
        pa = preact[u]
        sg = 1.0 / (1.0 + jnp.exp(-pa))
        gpre = (gh * sg * (1.0 + pa * (1.0 - sg))).astype(BF16)
        gm = mm(w[0], gpre)
        for q in range(4):
            cells[pl.ds(4 * u + q, width, stride=32), :] = gm[:, q * 128 : (q + 1) * 128]

    def backward_half(half):
        wait_for(sums.at[half, 0], sums_in.at[half, 0])
        backward(half, im // 2)
        for t in (1, 2, 3):
            wait_for(sums.at[half, 0], sums_in.at[half, t])
            sums_copy(
                half, (im + 8 - 2 * t) % 8, partner, fwd_out.at[half, t], fwd_in.at[half, t]
            ).start()

        @pl.loop(1, 4)
        def _(t):
            wait_for(sums.at[half, 0], fwd_in.at[half, t])
            backward(half, (im // 2 + 4 - t) % 4)

    for ch in range(chunks):
        wait_31(chunk, back_in.at[ch])
        unpack(ch)
    decode_half(0)
    for ch in range(chunks):
        wait_31(chunk, out_sem.at[ch])
        wait_low(chunk, out_sem.at[chunks + ch])
    sum_half(0)
    backward_half(0)
    fill_block()
    to_owners(ggrid, 0, own_width, gout_sem.at[chunks], gin_sem.at[chunks])
    wait_low(own_width, back_in.at[chunks])
    unpack_low()
    decode_half(1)
    sum_half(1)
    backward_half(1)
    fill_low()
    for ch in range(chunks):
        low_to_owners(ggrid_low, ch * chunk, chunk, gout_sem.at[ch], gin_sem.at[ch])

    @pl.loop(0, variables)
    def _(v):
        nll_all[v] = loss_rows[pl.ds(pl.multiple_of(v * 32, 32), own_rows), 0:own_columns]

    nll_copy = pltpu.make_async_copy(nll_all, nll, nll_sem)
    nll_copy.start()
    wait_31(own_width, gin_sem.at[chunks])
    for ch in range(chunks):
        wait_low(chunk, gin_sem.at[ch])
        spread_low(ggrid_low, ggrid, ch)

        @pl.loop(ch * chunk, (ch + 1) * chunk)
        def _(c):
            own = lane == ilon * own_width + c
            g = to_spectral(ggrid[c])
            gr, gi = g[:, 0:256], g[:, 256:512]
            sr, si = spectrum[c, :, 0:256], spectrum[c, :, 256:512]
            g_re = jnp.sum(jnp.where(keep, gr * sr + gi * si, 0.0), axis=1, keepdims=True)
            g_im = jnp.sum(jnp.where(keep, gi * sr - gr * si, 0.0), axis=1, keepdims=True)
            gsum[0] = gsum[0] + jnp.where(own, g_re, 0.0)
            gsum[1] = gsum[1] + jnp.where(own, g_im, 0.0)

    @pl.loop(1, 4)
    def _(o):
        lo = (ilon + o) % 4
        pltpu.make_async_remote_copy(
            gsum.at[:, pl.ds(pl.multiple_of(lo * 64, 64), 64), :],
            gsum_in.at[ilon],
            grad_out,
            grad_in,
            device_id=(im, ilat, lo),
            device_id_type=MESH_ID,
        ).start()

    gsum_in[ilon] = gsum[:, pl.ds(pl.multiple_of(ilon * 64, 64), 64), :]
    wait_for(gsum_in.at[pl.ds(0, 3)], grad_in)
    total = gsum_in[0] + gsum_in[1] + gsum_in[2] + gsum_in[3]
    for n, part in enumerate((grad_re, grad_im)):
        square[0:64] = total[n]
        part[0] = square[...].T[0:48, 0:60]

    for ch in range(chunks):
        wait_31(chunk, back_out.at[ch])
    wait_low(own_width, back_out.at[chunks])
    wait_31(own_width, gout_sem.at[chunks])
    for ch in range(chunks):
        wait_low(chunk, gout_sem.at[ch])
    nll_copy.wait()
    for half in range(2):
        wait_for(pred.at[half, pl.ds(0, 7)], pred_out.at[half])
        for t in range(4):
            wait_for(sums.at[half, 0], sums_out.at[half, t])
        for t in (1, 2, 3):
            wait_for(sums.at[half, 0], fwd_out.at[half, t])
    wait_for(weights.at[:, pl.ds(0, 192), :], filt_out)
    wait_for(gsum_in.at[pl.ds(0, 3)], grad_out)


def on_device(fields, targets, filt_re, filt_im, w_in, b_in, w_out, b_out):
    lat_pad, lon_pad = tables()
    lat = jnp.asarray(lat_pad, BF16)
    lat_t = jnp.asarray(lat_pad.T.copy(), BF16)
    lon = jnp.asarray(lon_pad, BF16)
    lon_t = jnp.asarray(lon_pad.T.copy(), BF16)
    anywhere = pl.BlockSpec(memory_space=pl.ANY)
    vmem = pl.BlockSpec(memory_space=pltpu.VMEM)
    dma = pltpu.SemaphoreType.DMA
    filt_re, filt_im = jnp.swapaxes(filt_re, 1, 2), jnp.swapaxes(filt_im, 1, 2)
    nll, grad_re, grad_im = pl.pallas_call(
        kernel,
        out_shape=(
            jax.ShapeDtypeStruct(targets.shape, F32),
            jax.ShapeDtypeStruct(filt_re.shape, F32),
            jax.ShapeDtypeStruct(filt_re.shape, F32),
        ),
        in_specs=[anywhere] * 12,
        out_specs=(anywhere, vmem, vmem),
        scratch_shapes=[
            pltpu.VMEM(fields.shape[1:], BF16),
            pltpu.VMEM(targets.shape, F32),
            pltpu.VMEM(filt_re.shape, F32),
            pltpu.VMEM(filt_im.shape, F32),
            pltpu.VMEM(w_in.shape, BF16),
            pltpu.VMEM(b_in.shape, F32),
            pltpu.VMEM(w_out.shape, BF16),
            pltpu.VMEM(b_out.shape, F32),
            pltpu.VMEM((256, 256), BF16),
            pltpu.VMEM((256, 256), BF16),
            pltpu.VMEM((512, 512), BF16),
            pltpu.VMEM((512, 512), BF16),
            pltpu.VMEM((80 * 32, 128), F32),
            pltpu.VMEM((80 * 32, 128), F32),
            pltpu.VMEM((2, 64, 128), F32),
            pltpu.VMEM((128, 128), F32),
            pltpu.VMEM((width, width), BF16),
            pltpu.VMEM((width, 128), F32),
            pltpu.VMEM((128, width), F32),
            pltpu.VMEM((width, 256), BF16),
            pltpu.VMEM((128, 128), F32),
            pltpu.VMEM((width * 32, 128), F32),
            pltpu.VMEM((8, width, 512), BF16),
            pltpu.VMEM((width, 16, 128), BF16),
            pltpu.VMEM((32, own_width * low, 128), BF16),
            pltpu.VMEM((own_width, 256, 512), BF16),
            pltpu.VMEM((32, own_width * low, 128), BF16),
            pltpu.VMEM((own_width, 128, 512), BF16),
            pltpu.VMEM((32, own_width * low, 128), BF16),
            pltpu.VMEM((width, 16, 128), BF16),
            pltpu.VMEM((32, own_width * low, 128), BF16),
            pltpu.VMEM((own_width, 256, 512), F32),
            pltpu.VMEM((8, width, 512), F32),
            pltpu.VMEM((2, 8, 80, 256), F32),
            pltpu.VMEM((2, 8, 80, 256), F32),
            pltpu.VMEM((2, 8, 2, 80, 256), F32),
            pltpu.VMEM((own_width, 256, 512), BF16),
            pltpu.VMEM((32, own_width * low, 128), BF16),
            pltpu.VMEM((4, 176, 128), F32),
            pltpu.VMEM(targets.shape, F32),
            pltpu.VMEM((2, 256, 128), F32),
            pltpu.VMEM((2, 256, 128), F32),
            pltpu.VMEM((4, 2, 64, 128), F32),
            pltpu.VMEM((width, 512), BF16),
            pltpu.VMEM((256, 512), BF16),
            dma((16,)),
            dma,
            dma((2 * chunks,)),
            dma((2 * chunks,)),
            dma((chunks + 1,)),
            dma((chunks + 1,)),
            dma((chunks + 1,)),
            dma((chunks + 1,)),
            dma((2,)),
            dma((2,)),
            dma((2, 4)),
            dma((2, 4)),
            dma((2, 4)),
            dma((2, 4)),
            dma,
            dma,
            dma,
            dma,
        ],
        compiler_params=pltpu.CompilerParams(
            collective_id=0, has_side_effects=True, vmem_limit_bytes=67043328
        ),
    )(fields, targets, filt_re, filt_im, w_in, b_in, w_out, b_out, lat, lat_t, lon, lon_t)
    return nll, jnp.swapaxes(grad_re, 1, 2), jnp.swapaxes(grad_im, 1, 2)


def solution(mesh):
    placed = (
        P("member", "lat", "lon", None),
        P(None, "lat", "lon"),
        P("member", "lon", "lat"),
        P("member", "lon", "lat"),
        P("member", None, None),
        P("member", None),
        P("member", None, None),
        P("member", None),
    )
    return jax.shard_map(
        on_device,
        mesh=mesh,
        in_specs=placed,
        out_specs=(P(None, "lat", "lon"), P("member", "lon", "lat"), P("member", "lon", "lat")),
        check_vma=False,
    )
```

```python
import functools

import jax
import jax.numpy as jnp
import numpy as np
from jax import lax
from jax.experimental import pallas as pl
from jax.experimental.pallas import tpu as pltpu
from jax.sharding import PartitionSpec as P

MESH_ID = pl.DeviceIdType.MESH
F32 = jnp.float32
BF16 = jnp.bfloat16

rows, columns, width, variables, members = 240, 480, 384, 73, 8
own_rows, own_columns, own_width = 30, 120, 12
low = 14
chunks = 3
chunk = own_width // chunks
variance_floor = 0.1


def tables():
    k = np.arange(rows, dtype=np.float64)[:, None]
    j = np.arange(rows, dtype=np.float64)[None, :]
    lat = np.where(k == 0, np.sqrt(1.0 / rows), np.sqrt(2.0 / rows)) * np.cos(
        np.pi * k * (j + 0.5) / rows
    )
    half = columns // 2
    place = np.arange(columns, dtype=np.int64)[:, None]
    order = np.arange(half, dtype=np.int64)[None, :]
    angle = 2.0 * np.pi * (place * order % columns).astype(np.float64) / columns
    scale = np.where(order == 0, np.sqrt(1.0 / columns), np.sqrt(2.0 / columns))
    kpad = (np.arange(rows) // 60) * 64 + np.arange(rows) % 60
    part, inside = np.arange(rows) // 30, np.arange(rows) % 30
    jpad = np.where(inside < 16, part * 16 + inside, 128 + part * 16 + inside - 16)
    lpad = (np.arange(columns) // 120) * 128 + np.arange(columns) % 120
    lat_pad = np.zeros((256, 256), np.float32)
    lat_pad[np.ix_(kpad, jpad)] = lat
    lon_pad = np.zeros((512, 512), np.float32)
    lon_pad[np.ix_(lpad, np.arange(half))] = scale * np.cos(angle)
    lon_pad[np.ix_(lpad, 256 + np.arange(half))] = -scale * np.sin(angle)
    return lat_pad, lon_pad


def mm(a, b):
    return jnp.dot(a, b, preferred_element_type=F32)


def logistic(v):
    return 0.5 * jnp.tanh(0.5 * v) + 0.5


def wait_for(ref, sem):
    pltpu.make_async_copy(ref, ref, sem).wait()


def kernel(
    fields_hbm, targets_hbm, fre_hbm, fim_hbm, w_hbm, b_hbm, wo_hbm, bo_hbm,
    lat_hbm, lat_t_hbm, lon_hbm, lon_t_hbm,
    nll, grad_re, grad_im,
    fields, targets, fre, fim, w, b, wo, bo, lat, lat_t, lon, lon_t,
    goal, loss_rows, filters, square, w_t, b_col, wo_pad, wo_t, bo_col,
    cells, fields_t, block, block_low, grid, grid_low, spatial, spatial_low, back, back_low,
    spectrum, preact, pred, pred_in, sums, ggrid, ggrid_low, line, nll_all,
    filters_in, weights, gsum, gsum_in, mixed, gpair,
    load_sem, nll_sem, out_sem, in_sem, back_out, back_in, gout_sem, gin_sem, pred_out, pred_in_sem,
    sums_out, sums_in, fwd_out, fwd_in, filt_out, filt_in, grad_out, grad_in,
):
    im = lax.axis_index("member")
    ilat = lax.axis_index("lat")
    ilon = lax.axis_index("lon")
    me = ilat * 4 + ilon
    partner = (im // 2) * 2 + 1 - im % 2

    def peer(o):
        y, z = ilat % 4, (ilat // 4) * 4 + ilon
        y2, z2 = (y + o % 4) % 4, (z + o // 4) % 8
        la, lo = (z2 // 4) * 4 + y2, z2 % 4
        return (im, la, lo), la, lo

    def at_member(m):
        return (m, ilat, ilon)

    def load_fields(i):
        part = pl.ds(i * 6, 6)
        return pltpu.make_async_copy(fields_hbm.at[0, part], fields.at[part], load_sem.at[i])

    later = [
        pltpu.make_async_copy(src, dst, load_sem.at[5 + i])
        for i, (src, dst) in enumerate(
            [
                (fre_hbm, fre), (fim_hbm, fim), (lat_hbm, lat), (lon_hbm, lon),
                (lat_t_hbm, lat_t), (lon_t_hbm, lon_t), (w_hbm, w), (b_hbm, b),
                (wo_hbm, wo), (bo_hbm, bo), (targets_hbm, targets),
            ]
        )
    ]
    for i in range(5):
        load_fields(i).start()
    for copy in later:
        copy.start()

    barrier = pltpu.get_barrier_semaphore()

    @pl.loop(1, 32)
    def _(o):
        pl.semaphore_signal(barrier, 1, device_id=peer(o)[0], device_id_type=MESH_ID)

    @pl.loop(1, 8)
    def _(o):
        pl.semaphore_signal(
            barrier, 1, device_id=at_member((im + o) % 8), device_id_type=MESH_ID
        )

    def grid_part(c0, n, la, lo):
        return (
            pl.ds(c0, n),
            pl.ds(pl.multiple_of(la * 16, 16), 16),
            pl.ds(pl.multiple_of(lo * 128, 128), 128),
        )

    def block_part(c0, n, la, lo):
        return (pl.ds((la * 4 + lo) * own_width + c0, n),)

    def low_part(c0, n, la, lo):
        return (la * 4 + lo, pl.ds(c0 * low, n * low))

    def exchange(src, src_part, dst, dst_part, c0, n, sem_out, sem_in):
        @pl.loop(1, 32)
        def _(o):
            dev, la, lo = peer(o)
            pltpu.make_async_remote_copy(
                src.at[src_part(c0, n, la, lo)],
                dst.at[dst_part(c0, n, ilat, ilon)],
                sem_out,
                sem_in,
                device_id=dev,
                device_id_type=MESH_ID,
            ).start()

        dst[dst_part(c0, n, ilat, ilon)] = src[src_part(c0, n, ilat, ilon)]

    def to_owners(target, c0, n, sem_out, sem_in):
        exchange(block, block_part, target, grid_part, c0, n, sem_out, sem_in)

    def low_to_owners(target, c0, n, sem_out, sem_in):
        exchange(block_low, low_part, target, low_part, c0, n, sem_out, sem_in)

    def wait_31(n, sem):
        wait_for(block.at[pl.ds(0, 31 * n)], sem)

    def wait_low(n, sem):
        wait_for(block_low.at[pl.ds(0, 31), pl.ds(0, n * low)], sem)

    def turn(j, q):
        x = fields[j].astype(F32)
        x = jnp.concatenate([x, jnp.zeros((8, width), F32)], axis=0).T
        cells[pl.ds(j, width, stride=32), :] = x
        fields_t[j // 4, :, q * 128 : (q + 1) * 128] = x.astype(BF16)

    def fill_block():
        @pl.loop(0, width // 8)
        def _(i):
            for c in range(8):
                part = cells[pl.ds(pl.multiple_of(i * 256 + c * 32, 32), 16), :]
                block[i * 8 + c] = part.astype(BF16)

    def fill_low():
        @pl.loop(0, 16)
        def _(i):
            for e in range(2):
                d = i * 2 + e
                for c in range(own_width):
                    first = pl.multiple_of((d * own_width + c) * 32 + 16, 16)
                    line[e, pl.ds(c * low, 16), :] = cells[pl.ds(first, 16), :]
                block_low[d] = line[e, 0 : own_width * low, :].astype(BF16)

    def spread_low(src, target, ch):
        @pl.loop(0, 8)
        def _(la):
            for lo in range(4):
                part = src[la * 4 + lo, pl.ds(ch * chunk * low, chunk * low)]
                line[lo, 0 : chunk * low, :] = part.astype(F32)
                for c in range(chunk):
                    target[
                        ch * chunk + c,
                        pl.ds(pl.multiple_of(128 + la * 16, 16), 16),
                        lo * 128 : (lo + 1) * 128,
                    ] = line[lo, pl.ds(c * low, 16), :].astype(BF16)

    line[...] = jnp.zeros_like(line)

    for i in range(3):
        load_fields(i).wait()

    @pl.loop(0, 4)
    def _(u):
        for q in range(4):
            turn(u * 4 + q, q)

    fill_block()

    for copy in later[:2]:
        copy.wait()
    filters[...] = jnp.zeros_like(filters)
    for lo in range(4):
        mine = slice(lo * own_width, (lo + 1) * own_width)
        filters[lo, 0:own_width, 0:60] = fre[0, mine, :]
        filters[lo, own_width : 2 * own_width, 0:60] = fim[0, mine, :]

    pl.semaphore_wait(barrier, 31 + 7)

    @pl.loop(1, 4)
    def _(o):
        lo = (ilon + o) % 4
        pltpu.make_async_remote_copy(
            filters.at[lo],
            filters_in.at[ilon],
            filt_out,
            filt_in,
            device_id=(im, ilat, lo),
            device_id_type=MESH_ID,
        ).start()

    filters_in[ilon] = filters[ilon]

    to_owners(grid, 0, chunk, out_sem.at[0], in_sem.at[0])

    for i in range(3, 5):
        load_fields(i).wait()

    @pl.loop(4, 7)
    def _(u):
        for q in range(4):
            turn(u * 4 + q, q)

    turn(28, 0)
    turn(29, 1)
    for j in (30, 31):
        cells[pl.ds(j, width, stride=32), :] = jnp.zeros((width, 128), F32)
    fields_t[7, :, 256:512] = jnp.zeros((width, 256), BF16)
    fill_low()
    for ch in range(chunks):
        if ch > 0:
            to_owners(grid, ch * chunk, chunk, out_sem.at[ch], in_sem.at[ch])
        low_to_owners(
            grid_low, ch * chunk, chunk, out_sem.at[chunks + ch], in_sem.at[chunks + ch]
        )

    for copy in later[2:]:
        copy.wait()

    w_t[...] = w[0].astype(F32).T.astype(BF16)
    b_col[...] = jnp.broadcast_to(b[...], (128, width)).T
    wo_pad[...] = jnp.zeros_like(wo_pad)
    wo_pad[0:variables, :] = wo[0].astype(F32)
    turned = wo_pad[...].T.astype(BF16)
    wo_t[:, 0:128] = turned
    wo_t[:, 128:256] = turned
    bo_col[...] = jnp.zeros_like(bo_col)
    bo_col[0:1, 0:variables] = bo[...]
    bo_col[...] = jnp.broadcast_to(bo_col[0:1, :], (128, 128)).T
    goal[...] = jnp.zeros_like(goal)

    @pl.loop(0, variables)
    def _(v):
        goal[pl.ds(pl.multiple_of(v * 32, 32), own_rows), 0:own_columns] = targets[v]

    gpair[...] = jnp.zeros_like(gpair)
    gsum[...] = jnp.zeros_like(gsum)
    wait_for(filters_in.at[pl.ds(0, 3)], filt_in)
    square[...] = jnp.zeros_like(square)
    for lo in range(4):
        square[0 : 2 * own_width] = filters_in[lo]
        weights[lo * 64 : (lo + 1) * 64] = square[...].T[0:64]

    lane = lax.broadcasted_iota(jnp.int32, (256, 128), 1)
    k_row = lax.broadcasted_iota(jnp.int32, (256, 256), 0)
    keep = (k_row // 64) * 60 + k_row % 64 >= lax.broadcasted_iota(jnp.int32, (256, 256), 1)

    def to_spectral(x):
        return mm(mm(lat[...], x).astype(BF16), lon[...])

    for ch in range(chunks):
        wait_31(chunk, in_sem.at[ch])
        wait_low(chunk, in_sem.at[chunks + ch])
        spread_low(grid_low, grid, ch)

        @pl.loop(ch * chunk, (ch + 1) * chunk)
        def _(c):
            both = weights[...]
            wr = jnp.sum(jnp.where(lane == c, both, 0.0), axis=1, keepdims=True)
            wi = jnp.sum(jnp.where(lane == own_width + c, both, 0.0), axis=1, keepdims=True)
            spectrum[c] = to_spectral(grid[c])
            sr, si = spectrum[c, :, 0:256], spectrum[c, :, 256:512]
            fr = jnp.where(keep, wr * sr - wi * si, 0.0).astype(BF16)
            fi = jnp.where(keep, wr * si + wi * sr, 0.0).astype(BF16)
            lon_back = mm(jnp.concatenate([fr, fi], axis=1), lon_t[...]).astype(BF16)
            spatial[c] = mm(lat_t[0:128, :], lon_back).astype(BF16)
            rest = mm(lat_t[128:256, :], lon_back)
            for la in range(8):
                for lo in range(4):
                    cells[pl.ds((la * 4 + lo) * 176 + c * low, 16), :] = rest[
                        la * 16 : la * 16 + 16, lo * 128 : lo * 128 + 128
                    ]

        exchange(
            spatial, grid_part, back, block_part, ch * chunk, chunk, back_out.at[ch], back_in.at[ch]
        )

    @pl.loop(0, 32)
    def _(d):
        part = cells[pl.ds(pl.multiple_of(d * 176, 16), own_width * low), :]
        spatial_low[d] = part.astype(BF16)

    exchange(
        spatial_low, low_part, back_low, low_part, 0, own_width,
        back_out.at[chunks], back_in.at[chunks],
    )

    def unpack(ch):
        @pl.loop(0, 32)
        def _(s):
            first = s * own_width + ch * chunk
            for c in range(chunk):
                cells[pl.ds(pl.multiple_of((first + c) * 32, 32), 16), :] = back[first + c].astype(F32)

    def unpack_low():
        @pl.loop(0, 16)
        def _(i):
            for e in range(2):
                s = i * 2 + e
                line[e, 0 : own_width * low, :] = back_low[s].astype(F32)
                for c in range(own_width):
                    first = pl.multiple_of((s * own_width + c) * 32 + 16, 16)
                    cells[pl.ds(first, 16), :] = line[e, pl.ds(c * low, 16), :]

    def decode(half, i):
        u = half * 4 + i
        for q in range(4):
            part = fields_t[u, :, q * 128 : (q + 1) * 128].astype(F32)
            part = part + cells[pl.ds(4 * u + q, width, stride=32), :]
            mixed[:, q * 128 : (q + 1) * 128] = part.astype(BF16)
        bias = b_col[...]
        pa = mm(w_t[...], mixed[...]) + jnp.concatenate([bias] * 4, axis=1)
        preact[u] = pa
        hidden = (pa * logistic(pa)).astype(BF16)
        bias = bo_col[0:80, :]
        out = mm(wo_pad[0:80, :].astype(BF16), hidden) + jnp.concatenate([bias] * 4, axis=1)
        pred[half, 2 * i] = out[:, 0:256]
        pred[half, 2 * i + 1] = out[:, 256:512]

    def decode_half(half):
        @pl.loop(0, 4)
        def _(o):
            i = (im // 2 + 1 + o) % 4
            decode(half, i)
            for e in range(2):
                r = 2 * i + e

                @pl.when(r != im)
                def _():
                    pltpu.make_async_remote_copy(
                        pred.at[half, r],
                        pred_in.at[half, im],
                        pred_out.at[half],
                        pred_in_sem.at[half],
                        device_id=at_member(r),
                        device_id_type=MESH_ID,
                    ).start()

    def sums_copy(half, index, m, sem_out, sem_in):
        return pltpu.make_async_remote_copy(
            sums.at[half, index],
            sums.at[half, index],
            sem_out,
            sem_in,
            device_id=at_member(m),
            device_id_type=MESH_ID,
        )

    def sum_half(half):
        pred_in[half, im] = pred[half, im]
        wait_for(pred.at[half, pl.ds(0, 7)], pred_in_sem.at[half])
        first = pred_in[half, 0]
        second = first * first
        for s in range(1, members):
            one = pred_in[half, s]
            first = first + one
            second = second + one * one
        sums[half, im, 0] = first
        sums[half, im, 1] = second
        for t in (1, 2, 3):
            sums_copy(
                half, im, (im + 2 * t) % 8, sums_out.at[half, t], sums_in.at[half, t]
            ).start()
        sums_copy(half, im, partner, sums_out.at[half, 0], sums_in.at[half, 0]).start()

    def backward(half, i):
        u = half * 4 + i
        mean, var = [
            jnp.concatenate([sums[half, 2 * i, n], sums[half, 2 * i + 1, n]], axis=1) / members
            for n in range(2)
        ]
        own_pred = jnp.concatenate([pred[half, 2 * i], pred[half, 2 * i + 1]], axis=1)
        var = var - mean * mean + variance_floor
        want = jnp.concatenate(
            [goal[pl.ds(4 * u + q, 80, stride=32), :] for q in range(4)], axis=1
        )
        res = want - mean
        inv = 1.0 / var
        loss = 0.5 * (jnp.log(var) + res * res * inv)
        for q in range(4):
            loss_rows[pl.ds(4 * u + q, 80, stride=32), :] = loss[:, q * 128 : (q + 1) * 128]
        gp = (
            -res * inv / members
            + (inv - res * res * inv * inv) * (own_pred - mean) / members
        ) / variables
        high = gp.astype(BF16)
        gpair[0:80, :] = high
        gpair[128:208, :] = (gp - high.astype(F32)).astype(BF16)
        gh = mm(wo_t[...], gpair[...])
        pa = preact[u]
        sg = logistic(pa)
        gpre = (gh * sg * (1.0 + pa * (1.0 - sg))).astype(BF16)
        gm = mm(w[0], gpre)
        for q in range(4):
            cells[pl.ds(4 * u + q, width, stride=32), :] = gm[:, q * 128 : (q + 1) * 128]

    def backward_half(half):
        wait_for(sums.at[half, 0], sums_in.at[half, 0])
        backward(half, im // 2)
        for t in (1, 2, 3):
            wait_for(sums.at[half, 0], sums_in.at[half, t])
            sums_copy(
                half, (im + 8 - 2 * t) % 8, partner, fwd_out.at[half, t], fwd_in.at[half, t]
            ).start()

        @pl.loop(1, 4)
        def _(t):
            wait_for(sums.at[half, 0], fwd_in.at[half, t])
            backward(half, (im // 2 + 4 - t) % 4)

    for ch in range(chunks):
        wait_31(chunk, back_in.at[ch])
        unpack(ch)
    decode_half(0)
    for ch in range(chunks):
        wait_31(chunk, out_sem.at[ch])
        wait_low(chunk, out_sem.at[chunks + ch])
    sum_half(0)
    backward_half(0)
    fill_block()
    to_owners(ggrid, 0, own_width, gout_sem.at[chunks], gin_sem.at[chunks])
    wait_low(own_width, back_in.at[chunks])
    unpack_low()
    decode_half(1)
    sum_half(1)
    backward_half(1)
    fill_low()
    for ch in range(chunks):
        low_to_owners(ggrid_low, ch * chunk, chunk, gout_sem.at[ch], gin_sem.at[ch])

    @pl.loop(0, variables)
    def _(v):
        nll_all[v] = loss_rows[pl.ds(pl.multiple_of(v * 32, 32), own_rows), 0:own_columns]

    nll_copy = pltpu.make_async_copy(nll_all, nll, nll_sem)
    nll_copy.start()
    wait_31(own_width, gin_sem.at[chunks])
    for ch in range(chunks):
        wait_low(chunk, gin_sem.at[ch])
        spread_low(ggrid_low, ggrid, ch)

        @pl.loop(ch * chunk, (ch + 1) * chunk)
        def _(c):
            g = to_spectral(ggrid[c])
            gr, gi = g[:, 0:256], g[:, 256:512]
            sr, si = spectrum[c, :, 0:256], spectrum[c, :, 256:512]
            g_re = jnp.sum(jnp.where(keep, gr * sr + gi * si, 0.0), axis=1, keepdims=True)
            g_im = jnp.sum(jnp.where(keep, gi * sr - gr * si, 0.0), axis=1, keepdims=True)
            both = jnp.where(lane == c, g_re, gsum[...])
            gsum[...] = jnp.where(lane == own_width + c, g_im, both)

    wait_for(filters.at[pl.ds(0, 3)], filt_out)
    for lo in range(4):
        square[0:64] = gsum[lo * 64 : (lo + 1) * 64]
        filters[lo] = square[...].T[0 : 2 * own_width]

    @pl.loop(1, 4)
    def _(o):
        lo = (ilon + o) % 4
        pltpu.make_async_remote_copy(
            filters.at[lo],
            gsum_in.at[ilon],
            grad_out,
            grad_in,
            device_id=(im, ilat, lo),
            device_id_type=MESH_ID,
        ).start()

    gsum_in[ilon] = filters[ilon]
    wait_for(gsum_in.at[pl.ds(0, 3)], grad_in)
    for lo in range(4):
        mine = slice(lo * own_width, (lo + 1) * own_width)
        grad_re[0, mine, :] = gsum_in[lo, 0:own_width, 0:60]
        grad_im[0, mine, :] = gsum_in[lo, own_width : 2 * own_width, 0:60]

    for ch in range(chunks):
        wait_31(chunk, back_out.at[ch])
    wait_low(own_width, back_out.at[chunks])
    wait_31(own_width, gout_sem.at[chunks])
    for ch in range(chunks):
        wait_low(chunk, gout_sem.at[ch])
    nll_copy.wait()
    for half in range(2):
        wait_for(pred.at[half, pl.ds(0, 7)], pred_out.at[half])
        for t in range(4):
            wait_for(sums.at[half, 0], sums_out.at[half, t])
        for t in (1, 2, 3):
            wait_for(sums.at[half, 0], fwd_out.at[half, t])
    wait_for(gsum_in.at[pl.ds(0, 3)], grad_out)


def on_device(fields, targets, filt_re, filt_im, w_in, b_in, w_out, b_out):
    lat_pad, lon_pad = tables()
    lat = jnp.asarray(lat_pad, BF16)
    lat_t = jnp.asarray(lat_pad.T.copy(), BF16)
    lon = jnp.asarray(lon_pad, BF16)
    lon_t = jnp.asarray(lon_pad.T.copy(), BF16)
    anywhere = pl.BlockSpec(memory_space=pl.ANY)
    vmem = pl.BlockSpec(memory_space=pltpu.VMEM)
    dma = pltpu.SemaphoreType.DMA
    filt_re, filt_im = jnp.swapaxes(filt_re, 1, 2), jnp.swapaxes(filt_im, 1, 2)
    nll, grad_re, grad_im = pl.pallas_call(
        kernel,
        out_shape=(
            jax.ShapeDtypeStruct(targets.shape, F32),
            jax.ShapeDtypeStruct(filt_re.shape, F32),
            jax.ShapeDtypeStruct(filt_re.shape, F32),
        ),
        in_specs=[anywhere] * 12,
        out_specs=(anywhere, vmem, vmem),
        scratch_shapes=[
            pltpu.VMEM(fields.shape[1:], BF16),
            pltpu.VMEM(targets.shape, F32),
            pltpu.VMEM(filt_re.shape, F32),
            pltpu.VMEM(filt_im.shape, F32),
            pltpu.VMEM(w_in.shape, BF16),
            pltpu.VMEM(b_in.shape, F32),
            pltpu.VMEM(w_out.shape, BF16),
            pltpu.VMEM(b_out.shape, F32),
            pltpu.VMEM((256, 256), BF16),
            pltpu.VMEM((256, 256), BF16),
            pltpu.VMEM((512, 512), BF16),
            pltpu.VMEM((512, 512), BF16),
            pltpu.VMEM((80 * 32, 128), F32),
            pltpu.VMEM((80 * 32, 128), F32),
            pltpu.VMEM((4, 2 * own_width, 128), F32),
            pltpu.VMEM((128, 128), F32),
            pltpu.VMEM((width, width), BF16),
            pltpu.VMEM((width, 128), F32),
            pltpu.VMEM((128, width), F32),
            pltpu.VMEM((width, 256), BF16),
            pltpu.VMEM((128, 128), F32),
            pltpu.VMEM((width * 32, 128), F32),
            pltpu.VMEM((8, width, 512), BF16),
            pltpu.VMEM((width, 16, 128), BF16),
            pltpu.VMEM((32, own_width * low, 128), BF16),
            pltpu.VMEM((own_width, 256, 512), BF16),
            pltpu.VMEM((32, own_width * low, 128), BF16),
            pltpu.VMEM((own_width, 128, 512), BF16),
            pltpu.VMEM((32, own_width * low, 128), BF16),
            pltpu.VMEM((width, 16, 128), BF16),
            pltpu.VMEM((32, own_width * low, 128), BF16),
            pltpu.VMEM((own_width, 256, 512), F32),
            pltpu.VMEM((8, width, 512), F32),
            pltpu.VMEM((2, 8, 80, 256), F32),
            pltpu.VMEM((2, 8, 80, 256), F32),
            pltpu.VMEM((2, 8, 2, 80, 256), F32),
            pltpu.VMEM((own_width, 256, 512), BF16),
            pltpu.VMEM((32, own_width * low, 128), BF16),
            pltpu.VMEM((4, 176, 128), F32),
            pltpu.VMEM(targets.shape, F32),
            pltpu.VMEM((4, 2 * own_width, 128), F32),
            pltpu.VMEM((256, 128), F32),
            pltpu.VMEM((256, 128), F32),
            pltpu.VMEM((4, 2 * own_width, 128), F32),
            pltpu.VMEM((width, 512), BF16),
            pltpu.VMEM((256, 512), BF16),
            dma((16,)),
            dma,
            dma((2 * chunks,)),
            dma((2 * chunks,)),
            dma((chunks + 1,)),
            dma((chunks + 1,)),
            dma((chunks + 1,)),
            dma((chunks + 1,)),
            dma((2,)),
            dma((2,)),
            dma((2, 4)),
            dma((2, 4)),
            dma((2, 4)),
            dma((2, 4)),
            dma,
            dma,
            dma,
            dma,
        ],
        compiler_params=pltpu.CompilerParams(
            collective_id=0, has_side_effects=True, vmem_limit_bytes=67043328
        ),
    )(fields, targets, filt_re, filt_im, w_in, b_in, w_out, b_out, lat, lat_t, lon, lon_t)
    return nll, jnp.swapaxes(grad_re, 1, 2), jnp.swapaxes(grad_im, 1, 2)


def solution(mesh):
    placed = (
        P("member", "lat", "lon", None),
        P(None, "lat", "lon"),
        P("member", "lon", "lat"),
        P("member", "lon", "lat"),
        P("member", None, None),
        P("member", None),
        P("member", None, None),
        P("member", None),
    )
    return jax.shard_map(
        on_device,
        mesh=mesh,
        in_specs=placed,
        out_specs=(P(None, "lat", "lon"), P("member", "lon", "lat"), P("member", "lon", "lat")),
        check_vma=False,
    )
```

```python
import functools

import jax
import jax.numpy as jnp
import numpy as np
from jax import lax
from jax.experimental import pallas as pl
from jax.experimental.pallas import tpu as pltpu
from jax.sharding import PartitionSpec as P

MESH_ID = pl.DeviceIdType.MESH
F32 = jnp.float32
BF16 = jnp.bfloat16

rows, columns, width, variables, members = 240, 480, 384, 73, 8
own_rows, own_columns, own_width = 30, 120, 12
low = 14
low_rows = own_width * low
sent_rows = low_rows - 8
chunks = 3
chunk = own_width // chunks
variance_floor = 0.1


def tables():
    k = np.arange(rows, dtype=np.float64)[:, None]
    j = np.arange(rows, dtype=np.float64)[None, :]
    lat = np.where(k == 0, np.sqrt(1.0 / rows), np.sqrt(2.0 / rows)) * np.cos(
        np.pi * k * (j + 0.5) / rows
    )
    half = columns // 2
    place = np.arange(columns, dtype=np.int64)[:, None]
    order = np.arange(half, dtype=np.int64)[None, :]
    angle = 2.0 * np.pi * (place * order % columns).astype(np.float64) / columns
    scale = np.where(order == 0, np.sqrt(1.0 / columns), np.sqrt(2.0 / columns))
    kpad = (np.arange(rows) // 60) * 64 + np.arange(rows) % 60
    part, inside = np.arange(rows) // 30, np.arange(rows) % 30
    jpad = np.where(inside < 16, part * 16 + inside, 128 + part * 16 + inside - 16)
    lpad = (np.arange(columns) // 120) * 128 + np.arange(columns) % 120
    lat_pad = np.zeros((256, 256), np.float32)
    lat_pad[np.ix_(kpad, jpad)] = lat
    lon_pad = np.zeros((512, 512), np.float32)
    lon_pad[np.ix_(lpad, np.arange(half))] = scale * np.cos(angle)
    lon_pad[np.ix_(lpad, 256 + np.arange(half))] = -scale * np.sin(angle)
    return lat_pad, lon_pad


def mm(a, b):
    return jnp.dot(a, b, preferred_element_type=F32)


def logistic(v):
    return 0.5 * jnp.tanh(0.5 * v) + 0.5


def wait_for(ref, sem):
    pltpu.make_async_copy(ref, ref, sem).wait()


def kernel(
    fields_hbm, targets_hbm, fre_hbm, fim_hbm, w_hbm, b_hbm, wo_hbm, bo_hbm,
    lat_hbm, lat_t_hbm, lon_hbm, lon_t_hbm,
    nll, grad_re, grad_im,
    fields, targets, fre, fim, w, b, wo, bo, lat, lat_t, lon, lon_t,
    goal, loss_rows, filters, square, w_t, b_col, wo_pad, wo_t, bo_col,
    cells, fields_t, block, block_low, grid, grid_low, spatial, spatial_low, back, back_low,
    spectrum, preact, pred, pred_in, sums, ggrid, ggrid_low, line, tail, nll_all,
    filters_in, weights, gsum, gsum_in, mixed, gpair,
    load_sem, nll_sem, out_sem, in_sem, back_out, back_in, gout_sem, gin_sem, pred_out, pred_in_sem,
    back_low_in, gin_low, sums_out, sums_in, fwd_out, fwd_in, filt_out, filt_in, grad_out, grad_in,
):
    im = lax.axis_index("member")
    ilat = lax.axis_index("lat")
    ilon = lax.axis_index("lon")
    me = ilat * 4 + ilon
    partner = (im // 2) * 2 + 1 - im % 2

    def peer(o, sign=1):
        o = (32 - o) % 32
        y, z = ilat % 4, (ilat // 4) * 4 + ilon
        turn_z = sign * ((o % 8 + 1) // 2) * (2 * (o % 2) - 1)
        y2, z2 = (y + sign * (o // 8) + 4) % 4, (z + turn_z + 8) % 8
        la, lo = (z2 // 4) * 4 + y2, z2 % 4
        return (im, la, lo), la, lo

    def source(o):
        _, la, lo = peer(o, -1)
        return la, lo

    def at_member(m):
        return (m, ilat, ilon)

    def load_fields(i):
        part = pl.ds(i * 6, 6)
        return pltpu.make_async_copy(fields_hbm.at[0, part], fields.at[part], load_sem.at[i])

    later = [
        pltpu.make_async_copy(src, dst, load_sem.at[5 + i])
        for i, (src, dst) in enumerate(
            [
                (fre_hbm, fre), (fim_hbm, fim), (lat_hbm, lat), (lon_hbm, lon),
                (lat_t_hbm, lat_t), (lon_t_hbm, lon_t), (w_hbm, w), (b_hbm, b),
                (wo_hbm, wo), (bo_hbm, bo), (targets_hbm, targets),
            ]
        )
    ]
    for i in range(5):
        load_fields(i).start()
    for copy in later:
        copy.start()

    barrier = pltpu.get_barrier_semaphore()

    @pl.loop(1, 32)
    def _(o):
        pl.semaphore_signal(barrier, 1, device_id=peer(o)[0], device_id_type=MESH_ID)

    @pl.loop(1, 8)
    def _(o):
        pl.semaphore_signal(
            barrier, 1, device_id=at_member((im + o) % 8), device_id_type=MESH_ID
        )

    def grid_part(c0, n, la, lo):
        return (
            pl.ds(c0, n),
            pl.ds(pl.multiple_of(la * 16, 16), 16),
            pl.ds(pl.multiple_of(lo * 128, 128), 128),
        )

    def block_part(c0, n, la, lo):
        return (pl.ds((la * 4 + lo) * own_width + c0, n),)

    def low_part(c0, n, la, lo):
        return (la * 4 + lo, pl.ds(c0 * low, min((c0 + n) * low, sent_rows) - c0 * low))

    def exchange(src, src_part, dst, dst_part, c0, n, sem_out, sem_in):
        @pl.loop(1, 32)
        def _(o):
            dev, la, lo = peer(o)
            pltpu.make_async_remote_copy(
                src.at[src_part(c0, n, la, lo)],
                dst.at[dst_part(c0, n, ilat, ilon)],
                sem_out,
                sem_in,
                device_id=dev,
                device_id_type=MESH_ID,
            ).start()

        dst[dst_part(c0, n, ilat, ilon)] = src[src_part(c0, n, ilat, ilon)]

    def to_owners(target, c0, n, sem_out, sem_in):
        exchange(block, block_part, target, grid_part, c0, n, sem_out, sem_in)

    def low_to_owners(target, c0, n, sem_out, sem_in):
        exchange(block_low, low_part, target, low_part, c0, n, sem_out, sem_in)

    def wait_31(n, sem):
        wait_for(block.at[pl.ds(0, 31 * n)], sem)

    def wait_low(c0, n, sem):
        wait_for(block_low.at[(pl.ds(0, 31), *low_part(c0, n, 0, 0)[1:])], sem)

    def turn(j, q):
        x = fields[j].astype(F32)
        x = jnp.concatenate([x, jnp.zeros((8, width), F32)], axis=0).T
        cells[pl.ds(j, width, stride=32), :] = x
        fields_t[j // 4, :, q * 128 : (q + 1) * 128] = x.astype(BF16)

    def fill_block():
        @pl.loop(0, width // 8)
        def _(i):
            for c in range(8):
                part = cells[pl.ds(pl.multiple_of(i * 256 + c * 32, 32), 16), :]
                block[i * 8 + c] = part.astype(BF16)

    lane8 = lax.broadcasted_iota(jnp.int32, (8, 128), 1)

    def fold(rows_of):
        last = rows_of[sent_rows:low_rows, :]
        for i in range(15):
            moved = pltpu.roll(last, (120 - 8 * i) % 128, 1)
            rows_of[8 * i : 8 * i + 8, :] = jnp.where(
                lane8 >= own_columns, moved, rows_of[8 * i : 8 * i + 8, :]
            )

    def unfold(rows_of, first, end):
        last = jnp.zeros((8, 128), F32)
        for i in range(first // 8, end // 8):
            part = rows_of[8 * i : 8 * i + 8, :].astype(F32)
            moved = pltpu.roll(part, (8 * i - 120) % 128, 1)
            last = jnp.where(lane8 // 8 == i, moved, last)
        return last

    def fill_low():
        @pl.loop(0, 16)
        def _(i):
            for e in range(2):
                d = i * 2 + e
                for c in range(own_width):
                    first = pl.multiple_of((d * own_width + c) * 32 + 16, 16)
                    line[e, pl.ds(c * low, 16), :] = cells[pl.ds(first, 16), :]
                fold(line.at[e])
                block_low[d] = line[e, 0:sent_rows, :].astype(BF16)

    def spread_low(src, target, ch, sems=None):
        first = ch * chunk * low
        sent = min(first + chunk * low, sent_rows) - first

        @pl.loop(0, 8)
        def _(i):
            for e in range(4):
                la, lo = source(i * 4 + e)
                s = la * 4 + lo
                if sems is not None:

                    @pl.when(i * 4 + e > 0)
                    def _():
                        wait_for(src.at[s, pl.ds(first, sent)], sems.at[s])

                line[e, 0:sent, :] = src[s, pl.ds(first, sent)].astype(F32)
                if ch == chunks - 2:
                    tail[s] = unfold(src.at[s], 0, first + sent)
                if ch == chunks - 1:
                    line[e, sent : sent + 8, :] = tail[s] + unfold(src.at[s], first, 120)
                for c in range(chunk):
                    target[
                        ch * chunk + c,
                        pl.ds(pl.multiple_of(128 + la * 16, 16), 16),
                        pl.ds(pl.multiple_of(lo * 128, 128), 128),
                    ] = line[e, pl.ds(c * low, 16), :].astype(BF16)

    line[...] = jnp.zeros_like(line)

    for i in range(3):
        load_fields(i).wait()

    @pl.loop(0, 4)
    def _(u):
        for q in range(4):
            turn(u * 4 + q, q)

    fill_block()

    for copy in later[:2]:
        copy.wait()
    filters[...] = jnp.zeros_like(filters)
    for lo in range(4):
        mine = slice(lo * own_width, (lo + 1) * own_width)
        filters[lo, 0:own_width, 0:60] = fre[0, mine, :]
        filters[lo, own_width : 2 * own_width, 0:60] = fim[0, mine, :]

    pl.semaphore_wait(barrier, 31 + 7)

    @pl.loop(1, 4)
    def _(o):
        lo = (ilon + o) % 4
        pltpu.make_async_remote_copy(
            filters.at[lo],
            filters_in.at[ilon],
            filt_out,
            filt_in,
            device_id=(im, ilat, lo),
            device_id_type=MESH_ID,
        ).start()

    filters_in[ilon] = filters[ilon]

    to_owners(grid, 0, chunk, out_sem.at[0], in_sem.at[0])

    for i in range(3, 5):
        load_fields(i).wait()

    @pl.loop(4, 7)
    def _(u):
        for q in range(4):
            turn(u * 4 + q, q)

    turn(28, 0)
    turn(29, 1)
    for j in (30, 31):
        cells[pl.ds(j, width, stride=32), :] = jnp.zeros((width, 128), F32)
    fields_t[7, :, 256:512] = jnp.zeros((width, 256), BF16)
    fill_low()
    for ch in range(chunks):
        if ch > 0:
            to_owners(grid, ch * chunk, chunk, out_sem.at[ch], in_sem.at[ch])
        low_to_owners(
            grid_low, ch * chunk, chunk, out_sem.at[chunks + ch], in_sem.at[chunks + ch]
        )

    for copy in later[2:]:
        copy.wait()

    w_t[...] = w[0].astype(F32).T.astype(BF16)
    b_col[...] = jnp.broadcast_to(b[...], (128, width)).T
    wo_pad[...] = jnp.zeros_like(wo_pad)
    wo_pad[0:variables, :] = wo[0].astype(F32)
    turned = wo_pad[...].T.astype(BF16)
    wo_t[:, 0:128] = turned
    wo_t[:, 128:256] = turned
    bo_col[...] = jnp.zeros_like(bo_col)
    bo_col[0:1, 0:variables] = bo[...]
    bo_col[...] = jnp.broadcast_to(bo_col[0:1, :], (128, 128)).T
    goal[...] = jnp.zeros_like(goal)

    @pl.loop(0, variables)
    def _(v):
        goal[pl.ds(pl.multiple_of(v * 32, 32), own_rows), 0:own_columns] = targets[v]

    gpair[...] = jnp.zeros_like(gpair)
    gsum[...] = jnp.zeros_like(gsum)
    wait_for(filters_in.at[pl.ds(0, 3)], filt_in)
    square[...] = jnp.zeros_like(square)
    for lo in range(4):
        square[0 : 2 * own_width] = filters_in[lo]
        weights[lo * 64 : (lo + 1) * 64] = square[...].T[0:64]

    lane = lax.broadcasted_iota(jnp.int32, (256, 128), 1)
    k_row = lax.broadcasted_iota(jnp.int32, (256, 256), 0)
    keep = (k_row // 64) * 60 + k_row % 64 >= lax.broadcasted_iota(jnp.int32, (256, 256), 1)

    def to_spectral(x):
        return mm(mm(lat[...], x).astype(BF16), lon[...])

    for ch in range(chunks):
        wait_31(chunk, in_sem.at[ch])
        wait_low(ch * chunk, chunk, in_sem.at[chunks + ch])
        spread_low(grid_low, grid, ch)

        @pl.loop(ch * chunk, (ch + 1) * chunk)
        def _(c):
            both = weights[...]
            wr = jnp.sum(jnp.where(lane == c, both, 0.0), axis=1, keepdims=True)
            wi = jnp.sum(jnp.where(lane == own_width + c, both, 0.0), axis=1, keepdims=True)
            spectrum[c] = to_spectral(grid[c])
            sr, si = spectrum[c, :, 0:256], spectrum[c, :, 256:512]
            fr = jnp.where(keep, wr * sr - wi * si, 0.0).astype(BF16)
            fi = jnp.where(keep, wr * si + wi * sr, 0.0).astype(BF16)
            lon_back = mm(jnp.concatenate([fr, fi], axis=1), lon_t[...]).astype(BF16)
            spatial[c] = mm(lat_t[0:128, :], lon_back).astype(BF16)
            rest = mm(lat_t[128:256, :], lon_back)
            for la in range(8):
                for lo in range(4):
                    cells[pl.ds((la * 4 + lo) * 176 + c * low, 16), :] = rest[
                        la * 16 : la * 16 + 16, lo * 128 : lo * 128 + 128
                    ]

        exchange(
            spatial, grid_part, back, block_part, ch * chunk, chunk, back_out.at[ch], back_in.at[ch]
        )

    @pl.loop(0, 16)
    def _(i):
        for e in range(2):
            d = i * 2 + e
            line[e, 0:low_rows, :] = cells[pl.ds(pl.multiple_of(d * 176, 16), low_rows), :]
            fold(line.at[e])
            spatial_low[d] = line[e, 0:sent_rows, :].astype(BF16)

    exchange(
        spatial_low, low_part, back_low, low_part, 0, own_width,
        back_out.at[chunks], back_low_in.at[me],
    )

    def unpack(ch):
        @pl.loop(0, 32)
        def _(s):
            first = s * own_width + ch * chunk
            for c in range(chunk):
                cells[pl.ds(pl.multiple_of((first + c) * 32, 32), 16), :] = back[first + c].astype(F32)

    def unpack_low():
        @pl.loop(0, 16)
        def _(i):
            for e in range(2):
                la, lo = source(i * 2 + e)
                s = la * 4 + lo

                @pl.when(i * 2 + e > 0)
                def _():
                    wait_for(back_low.at[s], back_low_in.at[s])

                line[e, 0:sent_rows, :] = back_low[s].astype(F32)
                line[e, sent_rows:low_rows, :] = unfold(back_low.at[s], 0, 120)
                for c in range(own_width):
                    first = pl.multiple_of((s * own_width + c) * 32 + 16, 16)
                    cells[pl.ds(first, 16), :] = line[e, pl.ds(c * low, 16), :]

    def decode(half, i):
        u = half * 4 + i
        for q in range(4):
            part = fields_t[u, :, q * 128 : (q + 1) * 128].astype(F32)
            part = part + cells[pl.ds(4 * u + q, width, stride=32), :]
            mixed[:, q * 128 : (q + 1) * 128] = part.astype(BF16)
        bias = b_col[...]
        pa = mm(w_t[...], mixed[...]) + jnp.concatenate([bias] * 4, axis=1)
        preact[u] = pa
        hidden = (pa * logistic(pa)).astype(BF16)
        bias = bo_col[0:80, :]
        out = mm(wo_pad[0:80, :].astype(BF16), hidden) + jnp.concatenate([bias] * 4, axis=1)
        pred[half, 2 * i] = out[:, 0:256]
        pred[half, 2 * i + 1] = out[:, 256:512]

    def decode_half(half):
        @pl.loop(0, 4)
        def _(o):
            i = (im // 2 + 1 + o) % 4
            decode(half, i)
            for e in range(2):
                r = 2 * i + e

                @pl.when(r != im)
                def _():
                    pltpu.make_async_remote_copy(
                        pred.at[half, r],
                        pred_in.at[half, im],
                        pred_out.at[half],
                        pred_in_sem.at[half],
                        device_id=at_member(r),
                        device_id_type=MESH_ID,
                    ).start()

    def sums_copy(half, index, m, sem_out, sem_in):
        return pltpu.make_async_remote_copy(
            sums.at[half, index],
            sums.at[half, index],
            sem_out,
            sem_in,
            device_id=at_member(m),
            device_id_type=MESH_ID,
        )

    def sum_half(half):
        pred_in[half, im] = pred[half, im]
        wait_for(pred.at[half, pl.ds(0, 7)], pred_in_sem.at[half])
        first = pred_in[half, 0]
        second = first * first
        for s in range(1, members):
            one = pred_in[half, s]
            first = first + one
            second = second + one * one
        sums[half, im, 0] = first
        sums[half, im, 1] = second
        sums_copy(half, im, partner, sums_out.at[half, 0], sums_in.at[half, 0]).start()
        for t in (1, 3, 2):
            sums_copy(
                half, im, (im + 2 * t) % 8, sums_out.at[half, t], sums_in.at[half, t]
            ).start()

    def backward(half, i):
        u = half * 4 + i
        mean, var = [
            jnp.concatenate([sums[half, 2 * i, n], sums[half, 2 * i + 1, n]], axis=1) / members
            for n in range(2)
        ]
        own_pred = jnp.concatenate([pred[half, 2 * i], pred[half, 2 * i + 1]], axis=1)
        var = var - mean * mean + variance_floor
        want = jnp.concatenate(
            [goal[pl.ds(4 * u + q, 80, stride=32), :] for q in range(4)], axis=1
        )
        res = want - mean
        inv = 1.0 / var
        loss = 0.5 * (jnp.log(var) + res * res * inv)
        for q in range(4):
            loss_rows[pl.ds(4 * u + q, 80, stride=32), :] = loss[:, q * 128 : (q + 1) * 128]
        gp = (
            -res * inv / members
            + (inv - res * res * inv * inv) * (own_pred - mean) / members
        ) / variables
        high = gp.astype(BF16)
        gpair[0:80, :] = high
        gpair[128:208, :] = (gp - high.astype(F32)).astype(BF16)
        gh = mm(wo_t[...], gpair[...])
        pa = preact[u]
        sg = logistic(pa)
        gpre = (gh * sg * (1.0 + pa * (1.0 - sg))).astype(BF16)
        gm = mm(w[0], gpre)
        for q in range(4):
            cells[pl.ds(4 * u + q, width, stride=32), :] = gm[:, q * 128 : (q + 1) * 128]

    def backward_half(half):
        def pass_on(t):
            wait_for(sums.at[half, 0], sums_in.at[half, t])
            sums_copy(
                half, (im + 8 - 2 * t) % 8, partner, fwd_out.at[half, t], fwd_in.at[half, t]
            ).start()

        @pl.loop(0, 4)
        def _(i):
            t = i + (i // 2) * (1 - 2 * (i % 2))

            @pl.when(i == 0)
            def _():
                wait_for(sums.at[half, 0], sums_in.at[half, 0])

            @pl.when(i == 1)
            def _():
                pass_on(1)
                pass_on(3)

            @pl.when(i == 2)
            def _():
                pass_on(2)

            @pl.when(i > 0)
            def _():
                wait_for(sums.at[half, 0], fwd_in.at[half, t])

            backward(half, (im // 2 + 4 - t) % 4)

    for ch in range(chunks):
        wait_31(chunk, back_in.at[ch])
        unpack(ch)
    decode_half(0)
    for ch in range(chunks):
        wait_31(chunk, out_sem.at[ch])
        wait_low(ch * chunk, chunk, out_sem.at[chunks + ch])
    sum_half(0)
    backward_half(0)
    fill_block()
    to_owners(ggrid, 0, own_width, gout_sem.at[chunks], gin_sem.at[chunks])
    unpack_low()
    decode_half(1)
    sum_half(1)
    backward_half(1)
    fill_low()
    for ch in range(chunks):
        arrival = gin_sem.at[ch] if ch < chunks - 1 else gin_low.at[me]
        low_to_owners(ggrid_low, ch * chunk, chunk, gout_sem.at[ch], arrival)

    @pl.loop(0, variables)
    def _(v):
        nll_all[v] = loss_rows[pl.ds(pl.multiple_of(v * 32, 32), own_rows), 0:own_columns]

    nll_copy = pltpu.make_async_copy(nll_all, nll, nll_sem)
    nll_copy.start()
    wait_31(own_width, gin_sem.at[chunks])
    for ch in range(chunks):
        if ch < chunks - 1:
            wait_low(ch * chunk, chunk, gin_sem.at[ch])
            spread_low(ggrid_low, ggrid, ch)
        else:
            spread_low(ggrid_low, ggrid, ch, gin_low)

        @pl.loop(ch * chunk, (ch + 1) * chunk)
        def _(c):
            g = to_spectral(ggrid[c])
            gr, gi = g[:, 0:256], g[:, 256:512]
            sr, si = spectrum[c, :, 0:256], spectrum[c, :, 256:512]
            g_re = jnp.sum(jnp.where(keep, gr * sr + gi * si, 0.0), axis=1, keepdims=True)
            g_im = jnp.sum(jnp.where(keep, gi * sr - gr * si, 0.0), axis=1, keepdims=True)
            both = jnp.where(lane == c, g_re, gsum[...])
            gsum[...] = jnp.where(lane == own_width + c, g_im, both)

    wait_for(filters.at[pl.ds(0, 3)], filt_out)
    for lo in range(4):
        square[0:64] = gsum[lo * 64 : (lo + 1) * 64]
        filters[lo] = square[...].T[0 : 2 * own_width]

    @pl.loop(1, 4)
    def _(o):
        lo = (ilon + o) % 4
        pltpu.make_async_remote_copy(
            filters.at[lo],
            gsum_in.at[ilon],
            grad_out,
            grad_in,
            device_id=(im, ilat, lo),
            device_id_type=MESH_ID,
        ).start()

    gsum_in[ilon] = filters[ilon]
    wait_for(gsum_in.at[pl.ds(0, 3)], grad_in)
    for lo in range(4):
        mine = slice(lo * own_width, (lo + 1) * own_width)
        grad_re[0, mine, :] = gsum_in[lo, 0:own_width, 0:60]
        grad_im[0, mine, :] = gsum_in[lo, own_width : 2 * own_width, 0:60]

    for ch in range(chunks):
        wait_31(chunk, back_out.at[ch])
    wait_low(0, own_width, back_out.at[chunks])
    wait_31(own_width, gout_sem.at[chunks])
    for ch in range(chunks):
        wait_low(ch * chunk, chunk, gout_sem.at[ch])
    nll_copy.wait()
    for half in range(2):
        wait_for(pred.at[half, pl.ds(0, 7)], pred_out.at[half])
        for t in range(4):
            wait_for(sums.at[half, 0], sums_out.at[half, t])
        for t in (1, 2, 3):
            wait_for(sums.at[half, 0], fwd_out.at[half, t])
    wait_for(gsum_in.at[pl.ds(0, 3)], grad_out)


def finish(nll_in, re_in, im_in, nll, grad_re, grad_im, nll_all, re, im, in_sem, out_sem):
    pieces = [(nll_in, nll_all, nll, pl.ds(i * 19, min(19, variables - i * 19))) for i in range(4)]
    pieces += [(re_in, re, grad_re, pl.ds(0, 1)), (im_in, im, grad_im, pl.ds(0, 1))]
    reads = [
        pltpu.make_async_copy(src.at[at], mid.at[at], in_sem.at[i])
        for i, (src, mid, _, at) in enumerate(pieces)
    ]
    writes = [
        pltpu.make_async_copy(mid.at[at], dst.at[at], out_sem.at[i])
        for i, (_, mid, dst, at) in enumerate(pieces)
    ]
    for read in reads:
        read.start()
    for read, write in zip(reads, writes):
        read.wait()
        write.start()
    for write in writes:
        write.wait()


def on_device(fields, targets, filt_re, filt_im, w_in, b_in, w_out, b_out):
    lat_pad, lon_pad = tables()
    lat = jnp.asarray(lat_pad, BF16)
    lat_t = jnp.asarray(lat_pad.T.copy(), BF16)
    lon = jnp.asarray(lon_pad, BF16)
    lon_t = jnp.asarray(lon_pad.T.copy(), BF16)
    anywhere = pl.BlockSpec(memory_space=pl.ANY)
    vmem = pl.BlockSpec(memory_space=pltpu.VMEM)
    dma = pltpu.SemaphoreType.DMA
    filt_re, filt_im = jnp.swapaxes(filt_re, 1, 2), jnp.swapaxes(filt_im, 1, 2)
    nll, grad_re, grad_im = pl.pallas_call(
        kernel,
        out_shape=(
            jax.ShapeDtypeStruct(targets.shape, F32),
            jax.ShapeDtypeStruct(filt_re.shape, F32),
            jax.ShapeDtypeStruct(filt_re.shape, F32),
        ),
        in_specs=[anywhere] * 12,
        out_specs=(anywhere, vmem, vmem),
        scratch_shapes=[
            pltpu.VMEM(fields.shape[1:], BF16),
            pltpu.VMEM(targets.shape, F32),
            pltpu.VMEM(filt_re.shape, F32),
            pltpu.VMEM(filt_im.shape, F32),
            pltpu.VMEM(w_in.shape, BF16),
            pltpu.VMEM(b_in.shape, F32),
            pltpu.VMEM(w_out.shape, BF16),
            pltpu.VMEM(b_out.shape, F32),
            pltpu.VMEM((256, 256), BF16),
            pltpu.VMEM((256, 256), BF16),
            pltpu.VMEM((512, 512), BF16),
            pltpu.VMEM((512, 512), BF16),
            pltpu.VMEM((80 * 32, 128), F32),
            pltpu.VMEM((80 * 32, 128), F32),
            pltpu.VMEM((4, 2 * own_width, 128), F32),
            pltpu.VMEM((128, 128), F32),
            pltpu.VMEM((width, width), BF16),
            pltpu.VMEM((width, 128), F32),
            pltpu.VMEM((128, width), F32),
            pltpu.VMEM((width, 256), BF16),
            pltpu.VMEM((128, 128), F32),
            pltpu.VMEM((width * 32, 128), F32),
            pltpu.VMEM((8, width, 512), BF16),
            pltpu.VMEM((width, 16, 128), BF16),
            pltpu.VMEM((32, sent_rows, 128), BF16),
            pltpu.VMEM((own_width, 256, 512), BF16),
            pltpu.VMEM((32, sent_rows, 128), BF16),
            pltpu.VMEM((own_width, 128, 512), BF16),
            pltpu.VMEM((32, sent_rows, 128), BF16),
            pltpu.VMEM((width, 16, 128), BF16),
            pltpu.VMEM((32, sent_rows, 128), BF16),
            pltpu.VMEM((own_width, 256, 512), F32),
            pltpu.VMEM((8, width, 512), F32),
            pltpu.VMEM((2, 8, 80, 256), F32),
            pltpu.VMEM((2, 8, 80, 256), F32),
            pltpu.VMEM((2, 8, 2, 80, 256), F32),
            pltpu.VMEM((own_width, 256, 512), BF16),
            pltpu.VMEM((32, sent_rows, 128), BF16),
            pltpu.VMEM((4, 176, 128), F32),
            pltpu.VMEM((32, 8, 128), F32),
            pltpu.VMEM(targets.shape, F32),
            pltpu.VMEM((4, 2 * own_width, 128), F32),
            pltpu.VMEM((256, 128), F32),
            pltpu.VMEM((256, 128), F32),
            pltpu.VMEM((4, 2 * own_width, 128), F32),
            pltpu.VMEM((width, 512), BF16),
            pltpu.VMEM((256, 512), BF16),
            dma((16,)),
            dma,
            dma((2 * chunks,)),
            dma((2 * chunks,)),
            dma((chunks + 1,)),
            dma((chunks + 1,)),
            dma((chunks + 1,)),
            dma((chunks + 1,)),
            dma((2,)),
            dma((2,)),
            dma((32,)),
            dma((32,)),
            dma((2, 4)),
            dma((2, 4)),
            dma((2, 4)),
            dma((2, 4)),
            dma,
            dma,
            dma,
            dma,
        ],
        compiler_params=pltpu.CompilerParams(
            collective_id=0, has_side_effects=True, vmem_limit_bytes=67043328
        ),
    )(fields, targets, filt_re, filt_im, w_in, b_in, w_out, b_out, lat, lat_t, lon, lon_t)
    shapes = (nll.shape, grad_re.shape, grad_im.shape)
    nll, grad_re, grad_im = pl.pallas_call(
        finish,
        out_shape=tuple(jax.ShapeDtypeStruct(shape, F32) for shape in shapes),
        in_specs=[anywhere] * 3,
        out_specs=(anywhere,) * 3,
        scratch_shapes=[pltpu.VMEM(shape, F32) for shape in shapes] + [dma((6,)), dma((6,))],
    )(nll, grad_re, grad_im)
    return nll, jnp.swapaxes(grad_re, 1, 2), jnp.swapaxes(grad_im, 1, 2)


def solution(mesh):
    placed = (
        P("member", "lat", "lon", None),
        P(None, "lat", "lon"),
        P("member", "lon", "lat"),
        P("member", "lon", "lat"),
        P("member", None, None),
        P("member", None),
        P("member", None, None),
        P("member", None),
    )
    return jax.shard_map(
        on_device,
        mesh=mesh,
        in_specs=placed,
        out_specs=(P(None, "lat", "lon"), P("member", "lon", "lat"), P("member", "lon", "lat")),
        check_vma=False,
    )
```
